512 devices in a mesh: frame: 64 (over x, z_lo, core), head: 8 (over z_hi, y).
Axes of the slice: x: 4, y: 4, z: 16 (z_hi: 2, z_lo: 8; z = z_hi * 8 + z_lo), core: 2. Of those that a mesh axis runs over, the one named last changes fastest.
Arguments:
- queries: bfloat16 [65536, 1024], P(('frame', 'head')), may hold values from -8 to 8
- key_vectors: bfloat16 [65536, 1024], P(('frame', 'head')), may hold values from -5 to 5
- value_vectors: bfloat16 [65536, 1024], P(('frame', 'head')), may hold values from -6 to 6
- tile_lists: int32 [8, 512, 20], P('head', 'frame'), may hold values from 0 to 511, as said below
- live_slots: int32 [8, 512], P('head', 'frame'), may hold values from 2 to 20
Outputs:
- attended: bfloat16 [65536, 1024], P(('frame', 'head'))
The draws below stay inside these ranges and needn't reach their ends.
Inputs may be any that keep to these rules, and one draw needn't show every extreme that they name: `tile_lists`: slot 0 of query tile t holds t; the slots below live_slots hold distinct tiles u with |u - t| <= 32; the other slots hold t.
All inputs are finite; a program needn't handle non-finite values.
Results may differ from the reference program's by a relative error of at most 0.0045.
Values may be sent and summed in bfloat16 or wider, within the bound.
A program may use at most 64 MiB of HBM per device.

```python
import math
import jax
import jax.numpy as jnp
from jax import lax

TILE = 128
HEAD_DIM = 128
SEL = 20
FRAME_TILES = 28
JITTER = 4
TILES_DEV = 8
TILES = 512
TOKENS = 65536
HEADS = 8
REACH = 32


def tile_plan(key):
    span_count = 2 * REACH + 1
    offsets = jnp.arange(span_count, dtype=jnp.int32) - REACH
    pattern = jax.random.randint(jax.random.fold_in(key, 31), (HEADS, 1, 1), 0, 2)
    nearby = jnp.abs(offsets) <= JITTER
    framed = jnp.abs(jnp.abs(offsets) - FRAME_TILES) <= JITTER
    eligible = jnp.where(pattern == 1, nearby | framed, True) & (offsets != 0)
    query_tile = jnp.arange(TILES, dtype=jnp.int32)[None, :, None]
    targets = jnp.broadcast_to(query_tile + offsets, (HEADS, TILES, span_count))
    inside = eligible & (targets >= 0) & (targets < TILES)
    noise = jax.random.randint(jax.random.fold_in(key, 32), (HEADS, TILES, span_count), 0, 2 ** 20)
    ranking = noise * span_count + offsets + REACH
    middle = query_tile == TILES // 2
    ranking = jnp.where(middle & (offsets == REACH), -2, ranking)
    ranking = jnp.where(middle & (offsets == -REACH), -1, ranking)
    ranking = jnp.where(inside, ranking, 2 ** 30 + offsets + REACH)
    ordering = jnp.argsort(ranking, axis=-1, stable=True)[:, :, :SEL - 1]
    picked = jnp.take_along_axis(targets, ordering, axis=-1)
    counted = jnp.sum(inside.astype(jnp.int32), axis=-1)
    plenty = jax.random.randint(jax.random.fold_in(key, 33), (HEADS, TILES), SEL - SEL // 4, SEL + 1)
    sparse_count = jax.random.randint(jax.random.fold_in(key, 34), (HEADS, TILES), 2, SEL // 2 + 1)
    living = jnp.where(pattern[:, :, 0] == 1, sparse_count, plenty)
    living = jnp.where(middle[:, :, 0], SEL, living)
    living = jnp.minimum(living, counted + 1)
    own_tile = jnp.broadcast_to(query_tile, (HEADS, TILES, 1))
    slots_all = jnp.concatenate([own_tile, picked], axis=-1)
    slot_ids = jnp.arange(SEL, dtype=jnp.int32)
    slots_all = jnp.where(slot_ids < living[:, :, None], slots_all, query_tile)
    return (slots_all.astype(jnp.int32), living.astype(jnp.int32))


def draw_tile_lists(key, part):
    return tile_plan(key)[0]


def draw_live_slots(key, part):
    return tile_plan(key)[1]


def draw_queries(key, part):
    dimensions = (TOKENS, HEADS * HEAD_DIM)
    values_drawn = 2.0 * jnp.clip(jax.random.normal(jax.random.fold_in(key, 42), dimensions, dtype=jnp.float32), -4.0, 4.0)
    return values_drawn.astype(jnp.bfloat16)


def draw_key_vectors(key, part):
    dimensions = (TOKENS, HEADS * HEAD_DIM)
    values_drawn = jnp.clip(jax.random.normal(jax.random.fold_in(key, 44), dimensions, dtype=jnp.float32), -5.0, 5.0)
    return values_drawn.astype(jnp.bfloat16)


def steps_of(key, shape, cuts, least, high):
    gain = 1.0
    for dim, parts in cuts:
        steps = jax.random.uniform(jax.random.fold_in(jax.random.fold_in(key, 6), dim), (parts,), jnp.float32, least / len(cuts), high / len(cuts))
        gain = gain * jnp.repeat(jnp.exp(steps), shape[dim] // parts).reshape((-1,) + (1,) * (len(shape) - 1 - dim))
    return gain


def centred(stream_key, dims, deviation, bound, cuts=(), held_as=jnp.bfloat16):
    values = jax.random.normal(stream_key, dims, jnp.float32) * deviation
    if len(cuts) > 0:
        values = steps_of(stream_key, dims, cuts, -0.22, 0.18) * values
    return jnp.clip(values, min=-bound, max=bound).astype(held_as)


def setup_inputs(seed: int = 0) -> dict:
    streams_of = jax.random.split(jax.random.key(seed), 6)
    return {
        "queries": draw_queries(jax.random.fold_in(streams_of[5], 71), 0),
        "key_vectors": draw_key_vectors(jax.random.fold_in(streams_of[5], 71), 0),
        "value_vectors": centred(streams_of[2], (TOKENS, HEADS * HEAD_DIM), 1.0, 6.0, ((0, 512),)),
        "tile_lists": draw_tile_lists(jax.random.fold_in(streams_of[5], 71), 0),
        "live_slots": draw_live_slots(jax.random.fold_in(streams_of[5], 71), 0),
    }


def masked_softmax(query_tile_rows, gathered_key_block, gathered_value_block, usable):
    softmax_scale = 1.0 / math.sqrt(query_tile_rows.shape[-1])
    logit_scores = jnp.einsum('mar,mxr->max', query_tile_rows.astype(jnp.float32), gathered_key_block.astype(jnp.float32)) * softmax_scale
    logit_scores = jnp.where(usable[:, None, :], logit_scores, -jnp.inf)
    highest = lax.optimization_barrier(jnp.max(logit_scores, axis=-1, keepdims=True))
    exponent = jnp.exp(logit_scores - highest)
    denominator = lax.optimization_barrier(jnp.sum(exponent, axis=-1, keepdims=True))
    attention_weights = lax.optimization_barrier(exponent.astype(jnp.bfloat16)).astype(jnp.float32)
    weighted_sum = jnp.einsum('fve,fez->fvz', attention_weights, gathered_value_block.astype(jnp.float32))
    return (weighted_sum / denominator).astype(jnp.bfloat16)

def reference(queries, key_vectors, value_vectors, tile_lists, live_slots):
    groups = TILES // TILES_DEV
    outputs = []
    for head_index in range(HEADS):
        first_col = head_index * HEAD_DIM
        query_tile_rows = lax.slice_in_dim(queries, first_col, first_col + HEAD_DIM, axis=1).reshape(groups, TILES_DEV, TILE, HEAD_DIM)
        key_tiles = lax.slice_in_dim(key_vectors, first_col, first_col + HEAD_DIM, axis=1).reshape(TILES, TILE, HEAD_DIM)
        value_tiles = lax.slice_in_dim(value_vectors, first_col, first_col + HEAD_DIM, axis=1).reshape(TILES, TILE, HEAD_DIM)
        chosen = tile_lists[head_index].reshape(groups, TILES_DEV, SEL)
        living = live_slots[head_index].reshape(groups, TILES_DEV)

        def one_group(pieces, key_tiles=key_tiles, value_tiles=value_tiles):
            group_queries, group_ids, group_live = pieces
            gathered_key_block = key_tiles[group_ids].reshape(TILES_DEV, SEL * TILE, HEAD_DIM)
            gathered_value_block = value_tiles[group_ids].reshape(TILES_DEV, SEL * TILE, HEAD_DIM)
            slot_ids = jnp.arange(SEL, dtype=jnp.int32)
            usable = jnp.repeat(slot_ids[None, :] < group_live[:, None], TILE, axis=1)
            return masked_softmax(group_queries, gathered_key_block, gathered_value_block, usable)
        result = lax.map(one_group, (query_tile_rows, chosen, living))
        outputs.append(result.reshape(TOKENS, HEAD_DIM))
    return jnp.concatenate(outputs, axis=1)
```

```python
import math

import jax
import jax.numpy as jnp
from jax import lax
from jax.experimental import pallas as pl
from jax.experimental.pallas import tpu as pltpu
from jax.sharding import PartitionSpec as P

TILE = 128
DIM = 128
SLOTS = 20
COLS = 32
PERX = 8
SUBS = 2
PIECE = 4 // SUBS
MESH = pl.DeviceIdType.MESH

DN1, DN2, UP1, UP2, SB0, SBD1, SBU1, SBD2, SBU2 = range(9)


def kernel(
    q_in, k_in, v_in, lists_in, live_in, out,
    kv, qs, os, scores, list_land, live_land, lists, live,
    a2a_send, a2a_recv, win_send, win_recv, out_send, out_recv, meta_send, meta_recv, meta_local,
):
    f, g = lax.axis_index("frame"), lax.axis_index("head")
    m, c = lax.div(f, 2), lax.rem(f, 2)
    x = lax.div(m, PERX)
    zh, y = lax.div(g, 4), lax.rem(g, 4)
    b = lax.rem(zh + x, 2)
    head = b * 4 + y

    def half_of(rel):
        return lax.rem(b + lax.div(lax.rem(m + rel + COLS, COLS), PERX), 2)

    def device(rel, core):
        return (lax.rem(m + rel + COLS, COLS) * 2 + core, half_of(rel) * 4 + y)

    up, down, sibling = device(1, c), device(-1, c), device(0, 1 - c)

    def owner(i):
        far = 1 - lax.div(i, 4)
        zh2 = lax.rem(zh + far, 2)
        y2 = lax.rem(y + lax.rem(i, 4) + (1 - far), 4)
        return zh2 * 4 + y2, lax.rem(zh2 + x, 2) * 4 + y2

    others = [owner(jnp.int32(i)) for i in range(7)]

    barrier = pltpu.get_barrier_semaphore()
    for target in [(f, o) for o, _ in others] + [up, down, sibling]:
        pl.semaphore_signal(barrier, inc=1, device_id=target, device_id_type=MESH)
    pl.semaphore_wait(barrier, 10)

    started = []

    def remote(src, dst, send, recv, target):
        copy = pltpu.make_async_remote_copy(
            src_ref=src, dst_ref=dst, send_sem=send, recv_sem=recv, device_id=target, device_id_type=MESH
        )
        copy.start()
        return copy

    def columns(h):
        return pl.ds(pl.multiple_of(h * DIM, DIM), DIM)

    slot0 = 32 + c * 8
    ins = (k_in, v_in, q_in)

    def landing(t, j):
        return qs.at[j] if t == 2 else kv.at[slot0 + j, t]

    def exchange(i, t):
        o, h = others[i]
        started.append(
            remote(ins[t].at[:, columns(h)], landing(t, g), a2a_send.at[i, t], a2a_recv.at[g, t], (f, o))
        )

    def arrived(t, j):
        dst = landing(t, j)
        pltpu.make_async_copy(dst, dst, a2a_recv.at[j, t]).wait()

    for i in range(4):
        exchange(i, 0)
        exchange(i, 1)
    for i in range(4, 7):
        exchange(i, 0)
        exchange(i, 1)
    for t in range(3):
        pltpu.make_async_copy(ins[t].at[:, columns(head)], landing(t, g), a2a_recv.at[g, t]).start()
    for i in range(4, 7):
        exchange(i, 2)

    across = (f, lax.rem(g + 4, 8))
    started.append(remote(lists_in, list_land, meta_send.at[0], meta_recv.at[0], across))
    started.append(remote(live_in, live_land, meta_send.at[1], meta_recv.at[1], across))
    own_lists = pltpu.make_async_copy(lists_in.at[0], lists.at[0], meta_local.at[0])
    own_live = pltpu.make_async_copy(live_in, live.at[pl.ds(0, 1)], meta_local.at[1])
    own_lists.start()
    own_live.start()

    def tiles(rel, core, o, s):
        first = lax.rem(half_of(rel) + o, 2) * 4 + s * PIECE
        return pl.ds((rel + 2) * 16 + core * 8 + first, PIECE)

    def window_copy(kind, rel_src, rel_dst, o, s, target):
        src = tiles(rel_src, c, o, s)
        first = src.start - (rel_src + 2) * 16 + (rel_dst + 2) * 16
        return pltpu.make_async_remote_copy(
            src_ref=kv.at[src],
            dst_ref=kv.at[pl.ds(first, PIECE)],
            send_sem=win_send.at[kind, o, s],
            recv_sem=win_recv.at[kind, o, s],
            device_id=target,
            device_id_type=MESH,
        )

    def pass_on(kind, rel_src, rel_dst, o, s, target):
        copy = window_copy(kind, rel_src, rel_dst, o, s, target)
        copy.start()
        started.append(copy)

    def window_wait(kind, rel, core, o, s):
        dst = kv.at[tiles(rel, core, o, s)]
        pltpu.make_async_copy(dst, dst, win_recv.at[kind, o, s]).wait()

    for o in range(2):
        for s in range(SUBS):
            for p in range(PIECE):
                j = lax.rem(zh + o, 2) * 4 + s * PIECE + p
                arrived(0, j)
                arrived(1, j)
            pass_on(DN1, 0, -1, o, s, up)
            pass_on(UP1, 0, 1, o, s, down)
            pass_on(SB0, 0, 0, o, s, sibling)
        if o == 1:
            for i in range(4):
                exchange(i, 2)
        for s in range(SUBS):
            window_wait(DN1, -1, c, o, s)
            pass_on(DN2, -1, -2, o, s, up)
            pass_on(SBD1, -1, -1, o, s, sibling)
            window_wait(UP1, 1, c, o, s)
            pass_on(UP2, 1, 2, o, s, down)
            pass_on(SBU1, 1, 1, o, s, sibling)

    for o in range(2):
        for s in range(SUBS):
            window_wait(DN2, -2, c, o, s)

            @pl.when(c == 1)
            def _():
                window_copy(SBD2, -2, -2, o, s, sibling).start()

            window_wait(UP2, 2, c, o, s)

            @pl.when(c == 0)
            def _():
                window_copy(SBU2, 2, 2, o, s, sibling).start()

    for o in range(2):
        for s in range(SUBS):
            for kind, rel in ((SB0, 0), (SBD1, -1), (SBU1, 1)):
                window_wait(kind, rel, 1 - c, o, s)

            @pl.when(c == 0)
            def _():
                window_wait(SBD2, -2, 1, o, s)
                window_copy(SBU2, 2, 2, o, s, sibling).wait_send()

            @pl.when(c == 1)
            def _():
                window_wait(SBU2, 2, 0, o, s)
                window_copy(SBD2, -2, -2, o, s, sibling).wait_send()

    pltpu.make_async_copy(list_land, list_land, meta_recv.at[0]).wait()
    pltpu.make_async_copy(live_land, live_land, meta_recv.at[1]).wait()
    own_lists.wait()
    own_live.wait()
    crossed_lists = pltpu.make_async_copy(list_land.at[0], lists.at[1], meta_local.at[2])
    crossed_live = pltpu.make_async_copy(live_land, live.at[pl.ds(1, 1)], meta_local.at[3])
    crossed_lists.start()
    crossed_live.start()
    crossed_lists.wait()
    crossed_live.wait()

    odd = lax.rem(x, 2)
    base = (m - 2) * 16
    factor = math.log2(math.e) / math.sqrt(DIM)

    def attend(i, carry):
        j, _ = owner(i)
        arrived(2, j)
        query = qs[j]
        ids = [jnp.clip(lists[odd, j, s] - base, 0, 79) for s in range(SLOTS)]
        count = live[odd, j]
        peak = jnp.full((TILE, 2 * TILE), -jnp.inf, jnp.float32)
        for s in range(0, SLOTS, 2):
            pair = jnp.concatenate([kv[ids[s], 0], kv[ids[s + 1], 0]], axis=0)
            raw = lax.dot_general(query, pair, (((1,), (1,)), ((), ())), preferred_element_type=jnp.float32)
            scores[s // 2] = raw
            peak = jnp.maximum(peak, raw)
        top = jnp.max(peak, axis=1, keepdims=True) * factor
        total = jnp.zeros((TILE, 2 * TILE), jnp.float32)
        acc = jnp.zeros((TILE, DIM), jnp.float32)
        lane = lax.broadcasted_iota(jnp.int32, (1, 2 * TILE), 1)
        for s in range(0, SLOTS, 2):
            dead = jnp.where(s + lax.div(lane, TILE) < count, 0.0, jnp.inf)
            weight = jnp.exp2(scores[s // 2] * factor - (top + dead))
            total = total + weight
            pair = jnp.concatenate([kv[ids[s], 1], kv[ids[s + 1], 1]], axis=0)
            acc = acc + jnp.dot(weight.astype(jnp.bfloat16), pair, preferred_element_type=jnp.float32)
        os[j] = (acc / jnp.sum(total, axis=1, keepdims=True)).astype(jnp.bfloat16)

        @pl.when(i < 7)
        def _():
            remote(os.at[j], out.at[:, columns(head)], out_send.at[j], out_recv.at[g], (f, j))

        @pl.when(i == 7)
        def _():
            pltpu.make_async_copy(os.at[j], out.at[:, columns(head)], out_recv.at[g]).start()

        return carry

    lax.fori_loop(0, 8, attend, 0)

    for copy in started:
        copy.wait_send()
    for o, _ in others:
        pltpu.make_async_copy(os.at[o], os.at[o], out_send.at[o]).wait()
    for o, h in others + [(g, head)]:
        dst = out.at[:, columns(h)]
        pltpu.make_async_copy(dst, dst, out_recv.at[o]).wait()


def body(queries, key_vectors, value_vectors, tile_lists, live_slots):
    dma = pltpu.SemaphoreType.DMA
    hbm = pl.BlockSpec(memory_space=pl.ANY)
    bf16, i32 = jnp.bfloat16, jnp.int32
    return pl.pallas_call(
        kernel,
        out_shape=jax.ShapeDtypeStruct(queries.shape, queries.dtype),
        in_specs=[hbm] * 5,
        out_specs=hbm,
        scratch_shapes=[
            pltpu.VMEM((80, 2, TILE, DIM), bf16),
            pltpu.VMEM((8, TILE, DIM), bf16),
            pltpu.VMEM((8, TILE, DIM), bf16),
            pltpu.VMEM((SLOTS // 2, TILE, 2 * TILE), jnp.float32),
            pltpu.VMEM(tile_lists.shape, i32),
            pltpu.VMEM(live_slots.shape, i32),
            pltpu.SMEM((2,) + tile_lists.shape[1:], i32),
            pltpu.SMEM((2, live_slots.shape[1]), i32),
            dma((7, 3)),
            dma((8, 3)),
            dma((9, 2, SUBS)),
            dma((9, 2, SUBS)),
            dma((8,)),
            dma((8,)),
            dma((2,)),
            dma((2,)),
            dma((4,)),
        ],
        compiler_params=pltpu.CompilerParams(
            collective_id=0, has_side_effects=True, vmem_limit_bytes=32 << 20
        ),
    )(queries, key_vectors, value_vectors, tile_lists, live_slots)


def solution(mesh):
    placed = (
        P(("frame", "head"), None),
        P(("frame", "head"), None),
        P(("frame", "head"), None),
        P("head", "frame", None),
        P("head", "frame"),
    )
    return jax.shard_map(
        body, mesh=mesh, in_specs=placed, out_specs=P(("frame", "head"), None), check_vma=False
    )
```

```python
import math

import jax
import jax.numpy as jnp
from jax import lax
from jax.experimental import pallas as pl
from jax.experimental.pallas import tpu as pltpu
from jax.sharding import PartitionSpec as P

TILE = 128
DIM = 128
SLOTS = 20
COLS = 32
PERX = 8
SUBS = 2
PIECE = 4 // SUBS
MESH = pl.DeviceIdType.MESH

DN1, DN2, UP1, UP2, SB0, SBD1, SBU1, SBD2, SBU2 = range(9)


def kernel(
    q_in, k_in, v_in, lists_in, live_in, out,
    kv, qs, os, scores, list_land, live_land, lists, live,
    a2a_send, a2a_recv, win_send, win_recv, out_send, out_recv, meta_send, meta_recv, meta_local,
):
    f, g = lax.axis_index("frame"), lax.axis_index("head")
    m, c = lax.div(f, 2), lax.rem(f, 2)
    x = lax.div(m, PERX)
    zh, y = lax.div(g, 4), lax.rem(g, 4)
    b = lax.rem(zh + x, 2)
    head = b * 4 + y

    def half_of(rel):
        return lax.rem(b + lax.div(lax.rem(m + rel + COLS, COLS), PERX), 2)

    def device(rel, core):
        return (lax.rem(m + rel + COLS, COLS) * 2 + core, half_of(rel) * 4 + y)

    up, down, sibling = device(1, c), device(-1, c), device(0, 1 - c)

    def owner(i):
        far = 1 - lax.div(i, 4)
        zh2 = lax.rem(zh + far, 2)
        y2 = lax.rem(y + lax.rem(i, 4) + (1 - far), 4)
        return zh2 * 4 + y2, lax.rem(zh2 + x, 2) * 4 + y2

    others = [owner(jnp.int32(i)) for i in range(7)]

    barrier = pltpu.get_barrier_semaphore()
    for target in [(f, o) for o, _ in others] + [up, down, sibling]:
        pl.semaphore_signal(barrier, inc=1, device_id=target, device_id_type=MESH)
    pl.semaphore_wait(barrier, 10)

    started = []

    def remote(src, dst, send, recv, target):
        copy = pltpu.make_async_remote_copy(
            src_ref=src, dst_ref=dst, send_sem=send, recv_sem=recv, device_id=target, device_id_type=MESH
        )
        copy.start()
        return copy

    def columns(h):
        return pl.ds(pl.multiple_of(h * DIM, DIM), DIM)

    slot0 = 32 + c * 8
    ins = (k_in, v_in, q_in)

    def landing(t, j):
        return qs.at[j] if t == 2 else kv.at[slot0 + j, t]

    def exchange(i, t):
        o, h = others[i]
        started.append(
            remote(ins[t].at[:, columns(h)], landing(t, g), a2a_send.at[i, t], a2a_recv.at[g, t], (f, o))
        )

    def arrived(t, j):
        dst = landing(t, j)
        pltpu.make_async_copy(dst, dst, a2a_recv.at[j, t]).wait()

    for i in range(4):
        exchange(i, 0)
        exchange(i, 1)
    for i in range(4, 7):
        exchange(i, 0)
        exchange(i, 1)
    for t in range(3):
        pltpu.make_async_copy(ins[t].at[:, columns(head)], landing(t, g), a2a_recv.at[g, t]).start()
    for i in range(4, 7):
        exchange(i, 2)

    across = (f, lax.rem(g + 4, 8))
    started.append(remote(lists_in, list_land, meta_send.at[0], meta_recv.at[0], across))
    started.append(remote(live_in, live_land, meta_send.at[1], meta_recv.at[1], across))
    own_lists = pltpu.make_async_copy(lists_in.at[0], lists.at[0], meta_local.at[0])
    own_live = pltpu.make_async_copy(live_in, live.at[pl.ds(0, 1)], meta_local.at[1])
    own_lists.start()
    own_live.start()

    def tiles(rel, core, o, s):
        first = lax.rem(half_of(rel) + o, 2) * 4 + s * PIECE
        return pl.ds((rel + 2) * 16 + core * 8 + first, PIECE)

    def window_copy(kind, rel_src, rel_dst, o, s, target):
        src = tiles(rel_src, c, o, s)
        first = src.start - (rel_src + 2) * 16 + (rel_dst + 2) * 16
        return pltpu.make_async_remote_copy(
            src_ref=kv.at[src],
            dst_ref=kv.at[pl.ds(first, PIECE)],
            send_sem=win_send.at[kind, o, s],
            recv_sem=win_recv.at[kind, o, s],
            device_id=target,
            device_id_type=MESH,
        )

    def pass_on(kind, rel_src, rel_dst, o, s, target):
        copy = window_copy(kind, rel_src, rel_dst, o, s, target)
        copy.start()
        started.append(copy)

    def window_wait(kind, rel, core, o, s):
        dst = kv.at[tiles(rel, core, o, s)]
        pltpu.make_async_copy(dst, dst, win_recv.at[kind, o, s]).wait()

    for o in range(2):
        for s in range(SUBS):
            for p in range(PIECE):
                j = lax.rem(zh + o, 2) * 4 + s * PIECE + p
                arrived(0, j)
                arrived(1, j)
            pass_on(DN1, 0, -1, o, s, up)
            pass_on(UP1, 0, 1, o, s, down)
            pass_on(SB0, 0, 0, o, s, sibling)
        for s in range(SUBS):
            window_wait(DN1, -1, c, o, s)
            pass_on(DN2, -1, -2, o, s, up)
            pass_on(SBD1, -1, -1, o, s, sibling)
            window_wait(UP1, 1, c, o, s)
            pass_on(UP2, 1, 2, o, s, down)
            pass_on(SBU1, 1, 1, o, s, sibling)

    for i in range(4):
        exchange(i, 2)

    for o in range(2):
        for s in range(SUBS):
            window_wait(DN2, -2, c, o, s)

            @pl.when(c == 1)
            def _():
                window_copy(SBD2, -2, -2, o, s, sibling).start()

            window_wait(UP2, 2, c, o, s)

            @pl.when(c == 0)
            def _():
                window_copy(SBU2, 2, 2, o, s, sibling).start()

    for o in range(2):
        for s in range(SUBS):
            for kind, rel in ((SB0, 0), (SBD1, -1), (SBU1, 1)):
                window_wait(kind, rel, 1 - c, o, s)

            @pl.when(c == 0)
            def _():
                window_wait(SBD2, -2, 1, o, s)
                window_copy(SBU2, 2, 2, o, s, sibling).wait_send()

            @pl.when(c == 1)
            def _():
                window_wait(SBU2, 2, 0, o, s)
                window_copy(SBD2, -2, -2, o, s, sibling).wait_send()

    pltpu.make_async_copy(list_land, list_land, meta_recv.at[0]).wait()
    pltpu.make_async_copy(live_land, live_land, meta_recv.at[1]).wait()
    own_lists.wait()
    own_live.wait()
    crossed_lists = pltpu.make_async_copy(list_land.at[0], lists.at[1], meta_local.at[2])
    crossed_live = pltpu.make_async_copy(live_land, live.at[pl.ds(1, 1)], meta_local.at[3])
    crossed_lists.start()
    crossed_live.start()
    crossed_lists.wait()
    crossed_live.wait()

    odd = lax.rem(x, 2)
    base = (m - 2) * 16
    factor = math.log2(math.e) / math.sqrt(DIM)

    def attend(i, carry):
        j, _ = owner(i)
        arrived(2, j)
        query = qs[j]
        ids = [jnp.clip(lists[odd, j, s] - base, 0, 79) for s in range(SLOTS)]
        count = live[odd, j]
        peak = jnp.full((TILE, 2 * TILE), -jnp.inf, jnp.float32)
        for s in range(0, SLOTS, 2):
            pair = jnp.concatenate([kv[ids[s], 0], kv[ids[s + 1], 0]], axis=0)
            raw = lax.dot_general(query, pair, (((1,), (1,)), ((), ())), preferred_element_type=jnp.float32)
            scores[s // 2] = raw
            peak = jnp.maximum(peak, raw)
        top = jnp.max(peak, axis=1, keepdims=True) * factor
        total = jnp.zeros((TILE, 2 * TILE), jnp.float32)
        acc = jnp.zeros((TILE, DIM), jnp.float32)
        lane = lax.broadcasted_iota(jnp.int32, (1, 2 * TILE), 1)
        for s in range(0, SLOTS, 2):
            dead = jnp.where(s + lax.div(lane, TILE) < count, 0.0, jnp.inf)
            weight = jnp.exp2(scores[s // 2] * factor - (top + dead))
            total = total + weight
            pair = jnp.concatenate([kv[ids[s], 1], kv[ids[s + 1], 1]], axis=0)
            acc = acc + jnp.dot(weight.astype(jnp.bfloat16), pair, preferred_element_type=jnp.float32)
        os[j] = (acc / jnp.sum(total, axis=1, keepdims=True)).astype(jnp.bfloat16)

        @pl.when(i < 7)
        def _():
            remote(os.at[j], out.at[:, columns(head)], out_send.at[j], out_recv.at[g], (f, j))

        @pl.when(i == 7)
        def _():
            pltpu.make_async_copy(os.at[j], out.at[:, columns(head)], out_recv.at[g]).start()

        return carry

    lax.fori_loop(0, 8, attend, 0)

    for copy in started:
        copy.wait_send()
    for o, _ in others:
        pltpu.make_async_copy(os.at[o], os.at[o], out_send.at[o]).wait()
    for o, h in others + [(g, head)]:
        dst = out.at[:, columns(h)]
        pltpu.make_async_copy(dst, dst, out_recv.at[o]).wait()


def body(queries, key_vectors, value_vectors, tile_lists, live_slots):
    dma = pltpu.SemaphoreType.DMA
    hbm = pl.BlockSpec(memory_space=pltpu.HBM)
    bf16, i32 = jnp.bfloat16, jnp.int32
    return pl.pallas_call(
        kernel,
        out_shape=jax.ShapeDtypeStruct(queries.shape, queries.dtype),
        in_specs=[hbm] * 5,
        out_specs=hbm,
        scratch_shapes=[
            pltpu.VMEM((80, 2, TILE, DIM), bf16),
            pltpu.VMEM((8, TILE, DIM), bf16),
            pltpu.VMEM((8, TILE, DIM), bf16),
            pltpu.VMEM((SLOTS // 2, TILE, 2 * TILE), jnp.float32),
            pltpu.VMEM(tile_lists.shape, i32),
            pltpu.VMEM(live_slots.shape, i32),
            pltpu.SMEM((2,) + tile_lists.shape[1:], i32),
            pltpu.SMEM((2, live_slots.shape[1]), i32),
            dma((7, 3)),
            dma((8, 3)),
            dma((9, 2, SUBS)),
            dma((9, 2, SUBS)),
            dma((8,)),
            dma((8,)),
            dma((2,)),
            dma((2,)),
            dma((4,)),
        ],
        compiler_params=pltpu.CompilerParams(
            collective_id=0, has_side_effects=True, vmem_limit_bytes=63 << 20
        ),
    )(queries, key_vectors, value_vectors, tile_lists, live_slots)


def solution(mesh):
    placed = (
        P(("frame", "head"), None),
        P(("frame", "head"), None),
        P(("frame", "head"), None),
        P("head", "frame", None),
        P("head", "frame"),
    )
    return jax.shard_map(
        body, mesh=mesh, in_specs=placed, out_specs=P(("frame", "head"), None), check_vma=False
    )
```

```python
import math

import jax
import jax.numpy as jnp
from jax import lax
from jax.experimental import pallas as pl
from jax.experimental.pallas import tpu as pltpu
from jax.sharding import PartitionSpec as P

TILE = 128
DIM = 128
SLOTS = 20
COLS = 32
PERX = 8
SUBS = 2
PIECE = 4 // SUBS
MESH = pl.DeviceIdType.MESH

DN1, DN2, UP1, UP2, SB0, SBD1, SBU1, SBD2, SBU2 = range(9)


def kernel(
    q_in, k_in, v_in, lists_in, live_in, out,
    kv, qs, os, scores, list_land, live_land, lists, live,
    a2a_send, a2a_recv, win_send, win_recv, out_send, out_recv, meta_send, meta_recv, meta_local,
    far_send, far_recv, chain_send, chain_recv, sib_send, sib_recv,
):
    f, g = lax.axis_index("frame"), lax.axis_index("head")
    m, c = lax.div(f, 2), lax.rem(f, 2)
    x = lax.div(m, PERX)
    zh, y = lax.div(g, 4), lax.rem(g, 4)
    b = lax.rem(zh + x, 2)
    head = b * 4 + y

    def half_of(rel):
        return lax.rem(b + lax.div(lax.rem(m + rel + COLS, COLS), PERX), 2)

    def device(rel, core):
        return (lax.rem(m + rel + COLS, COLS) * 2 + core, half_of(rel) * 4 + y)

    up, down, sibling = device(1, c), device(-1, c), device(0, 1 - c)

    def owner(i):
        far = 1 - lax.div(i, 4)
        zh2 = lax.rem(zh + far, 2)
        y2 = lax.rem(y + lax.rem(i, 4) + (1 - far), 4)
        return zh2 * 4 + y2, lax.rem(zh2 + x, 2) * 4 + y2

    def fixed_owner(i):
        far = 1 - i // 4
        zh2 = lax.rem(zh + far, 2)
        y2 = lax.rem(y + i % 4 + (1 - far), 4)
        return zh2 * 4 + y2, lax.rem(zh2 + x, 2) * 4 + y2

    others = [fixed_owner(i) for i in range(7)]

    def across_to(rel, y2):
        column = lax.rem(m + rel + COLS, COLS)
        return (column * 2 + c, lax.rem(1 - b + lax.div(column, PERX), 2) * 4 + y2)

    rows = [lax.rem(y + i, 4) for i in range(4)]
    barrier = pltpu.get_barrier_semaphore()
    for target in (
        [(f, o) for o, _ in others]
        + [up, down, sibling]
        + [across_to(rel, y2) for rel in (-2, 2) for y2 in rows]
    ):
        pl.semaphore_signal(barrier, inc=1, device_id=target, device_id_type=MESH)
    pl.semaphore_wait(barrier, 18)

    started = []

    def remote(src, dst, send, recv, target):
        copy = pltpu.make_async_remote_copy(
            src_ref=src, dst_ref=dst, send_sem=send, recv_sem=recv, device_id=target, device_id_type=MESH
        )
        copy.start()
        return copy

    def columns(h):
        return pl.ds(pl.multiple_of(h * DIM, DIM), DIM)

    slot0 = 32 + c * 8
    ins = (k_in, v_in, q_in)

    def landing(t, j):
        return qs.at[j] if t == 2 else kv.at[slot0 + j, t]

    def exchange(i, t):
        o, h = others[i]
        started.append(
            remote(ins[t].at[:, columns(h)], landing(t, g), a2a_send.at[i, t], a2a_recv.at[g, t], (f, o))
        )

    def arrived(t, j):
        dst = landing(t, j)
        pltpu.make_async_copy(dst, dst, a2a_recv.at[j, t]).wait()

    for i, y2 in enumerate(rows):
        for t, rel in ((0, 2), (1, -2)):
            src = ins[t].at[:, columns((1 - b) * 4 + y2)]
            dst = kv.at[(rel + 2) * 16 + c * 8 + g, t]
            started.append(remote(src, dst, far_send.at[i, t], far_recv.at[y, t], across_to(-rel, y2)))
    for i in range(4, 7):
        exchange(i, 0)
        exchange(i, 1)
    for t in range(3):
        pltpu.make_async_copy(ins[t].at[:, columns(head)], landing(t, g), a2a_recv.at[g, t]).start()
    for i in range(4, 7):
        exchange(i, 2)

    across = (f, lax.rem(g + 4, 8))
    started.append(remote(lists_in, list_land, meta_send.at[0], meta_recv.at[0], across))
    started.append(remote(live_in, live_land, meta_send.at[1], meta_recv.at[1], across))
    own_lists = pltpu.make_async_copy(lists_in.at[0], lists.at[0], meta_local.at[0])
    own_live = pltpu.make_async_copy(live_in, live.at[pl.ds(0, 1)], meta_local.at[1])
    own_lists.start()
    own_live.start()

    def first_tile(rel, o, s):
        return lax.rem(half_of(rel) + o, 2) * 4 + s * PIECE

    def tiles(rel, core, o, s):
        return pl.ds((rel + 2) * 16 + core * 8 + first_tile(rel, o, s), PIECE)

    def window_copy(kind, rel_src, rel_dst, o, s, target):
        src = tiles(rel_src, c, o, s)
        first = src.start - (rel_src + 2) * 16 + (rel_dst + 2) * 16
        return pltpu.make_async_remote_copy(
            src_ref=kv.at[src],
            dst_ref=kv.at[pl.ds(first, PIECE)],
            send_sem=win_send.at[kind, o, s],
            recv_sem=win_recv.at[kind, o, s],
            device_id=target,
            device_id_type=MESH,
        )

    def pass_on(kind, rel_src, rel_dst, o, s, target):
        copy = window_copy(kind, rel_src, rel_dst, o, s, target)
        copy.start()
        started.append(copy)

    def window_wait(kind, rel, core, o, s):
        dst = kv.at[tiles(rel, core, o, s)]
        pltpu.make_async_copy(dst, dst, win_recv.at[kind, o, s]).wait()

    def own(o, s):
        for p in range(PIECE):
            j = first_tile(0, o, s) + p
            arrived(0, j)
            arrived(1, j)
        pass_on(DN1, 0, -1, o, s, up)
        pass_on(UP1, 0, 1, o, s, down)
        pass_on(SB0, 0, 0, o, s, sibling)

    def then(o, s):
        window_wait(DN1, -1, c, o, s)
        pass_on(DN2, -1, -2, o, s, up)
        pass_on(SBD1, -1, -1, o, s, sibling)
        window_wait(UP1, 1, c, o, s)
        pass_on(UP2, 1, 2, o, s, down)
        pass_on(SBU1, 1, 1, o, s, sibling)

    def chain_tiles(rel, core, t, s, to):
        return kv.at[pl.ds((to + 2) * 16 + core * 8 + first_tile(rel, 1, s), PIECE), t]

    def chain(stage):
        for s in range(SUBS):
            for t, rel, step, target in ((0, 2 - stage, -1, up), (1, stage - 2, 1, down)):
                if stage == 0:
                    for e in range(PIECE):
                        dst = kv.at[(rel + 2) * 16 + c * 8 + first_tile(rel, 1, s) + e, t]
                        pltpu.make_async_copy(dst, dst, far_recv.at[s * PIECE + e, t]).wait()
                else:
                    dst = chain_tiles(rel, c, t, s, rel)
                    pltpu.make_async_copy(dst, dst, chain_recv.at[stage - 1, t, s]).wait()
                if stage < 4:
                    src, dst = chain_tiles(rel, c, t, s, rel), chain_tiles(rel, c, t, s, rel + step)
                    started.append(remote(src, dst, chain_send.at[stage, t, s], chain_recv.at[stage, t, s], target))
                if abs(rel) < 2:
                    share(stage, t, rel, s).start()
                else:
                    pl.when(c == (0 if rel == 2 else 1))(share(stage, t, rel, s).start)

    def share(stage, t, rel, s):
        src = chain_tiles(rel, c, t, s, rel)
        return pltpu.make_async_remote_copy(
            src_ref=src,
            dst_ref=src,
            send_sem=sib_send.at[stage, t, s],
            recv_sem=sib_recv.at[stage, t, s],
            device_id=sibling,
            device_id_type=MESH,
        )

    def shared(stage, t, rel, s):
        dst = chain_tiles(rel, 1 - c, t, s, rel)
        wait = pltpu.make_async_copy(dst, dst, sib_recv.at[stage, t, s]).wait
        if abs(rel) < 2:
            wait()
            share(stage, t, rel, s).wait_send()
        else:
            sender = c == (0 if rel == 2 else 1)
            pl.when(sender)(share(stage, t, rel, s).wait_send)
            pl.when(jnp.logical_not(sender))(wait)

    q_copies = [
        pltpu.make_async_remote_copy(
            src_ref=q_in.at[:, columns(h)],
            dst_ref=qs.at[g],
            send_sem=a2a_send.at[i, 2],
            recv_sem=a2a_recv.at[g, 2],
            device_id=(f, o),
            device_id_type=MESH,
        )
        for i, (o, h) in enumerate(others[:4])
    ]
    started.extend(q_copies)

    def q_far(*some):
        for i in some:
            q_copies[i].start()

    soon = lax.rem(m, PERX) < 3
    for s in range(SUBS):
        own(0, s)
    for s in range(SUBS):
        then(0, s)
    chain(0)
    chain(1)
    chain(2)

    chain(3)

    pl.when(soon)(lambda: q_far(0, 1, 2, 3))
    chain(4)

    pl.when(jnp.logical_not(soon))(lambda: q_far(0, 1, 2, 3))
    for o in (0,):
        for s in range(SUBS):
            window_wait(DN2, -2, c, o, s)

            @pl.when(c == 1)
            def _():
                window_copy(SBD2, -2, -2, o, s, sibling).start()

            window_wait(UP2, 2, c, o, s)

            @pl.when(c == 0)
            def _():
                window_copy(SBU2, 2, 2, o, s, sibling).start()

    for o in (0,):
        for s in range(SUBS):
            for kind, rel in ((SB0, 0), (SBD1, -1), (SBU1, 1)):
                window_wait(kind, rel, 1 - c, o, s)

            @pl.when(c == 0)
            def _():
                window_wait(SBD2, -2, 1, o, s)
                window_copy(SBU2, 2, 2, o, s, sibling).wait_send()

            @pl.when(c == 1)
            def _():
                window_wait(SBU2, 2, 0, o, s)
                window_copy(SBD2, -2, -2, o, s, sibling).wait_send()

    for stage in range(5):
        for s in range(SUBS):
            shared(stage, 0, 2 - stage, s)
            shared(stage, 1, stage - 2, s)

    pltpu.make_async_copy(list_land, list_land, meta_recv.at[0]).wait()
    pltpu.make_async_copy(live_land, live_land, meta_recv.at[1]).wait()
    own_lists.wait()
    own_live.wait()
    crossed_lists = pltpu.make_async_copy(list_land.at[0], lists.at[1], meta_local.at[2])
    crossed_live = pltpu.make_async_copy(live_land, live.at[pl.ds(1, 1)], meta_local.at[3])
    crossed_lists.start()
    crossed_live.start()
    crossed_lists.wait()
    crossed_live.wait()

    odd = lax.rem(x, 2)
    base = (m - 2) * 16
    factor = math.log2(math.e) / math.sqrt(DIM)

    turn = jnp.where(lax.rem(m, PERX) >= 3, 4, 0)

    def attend(i, carry):
        i = lax.rem(i + turn, 8)
        j, _ = owner(i)
        arrived(2, j)
        query = qs[j]
        ids = [jnp.clip(lists[odd, j, s] - base, 0, 79) for s in range(SLOTS)]
        count = live[odd, j]
        peak = jnp.full((TILE, 2 * TILE), -jnp.inf, jnp.float32)
        for s in range(0, SLOTS, 2):
            pair = jnp.concatenate([kv[ids[s], 0], kv[ids[s + 1], 0]], axis=0)
            raw = lax.dot_general(query, pair, (((1,), (1,)), ((), ())), preferred_element_type=jnp.float32)
            scores[s // 2] = raw
            peak = jnp.maximum(peak, raw)
        top = jnp.max(peak, axis=1, keepdims=True) * factor
        total = jnp.zeros((TILE, 2 * TILE), jnp.float32)
        acc = jnp.zeros((TILE, DIM), jnp.float32)
        lane = lax.broadcasted_iota(jnp.int32, (1, 2 * TILE), 1)
        for s in range(0, SLOTS, 2):
            dead = jnp.where(s + lax.div(lane, TILE) < count, 0.0, jnp.inf)
            weight = jnp.exp2(scores[s // 2] * factor - (top + dead))
            total = total + weight
            pair = jnp.concatenate([kv[ids[s], 1], kv[ids[s + 1], 1]], axis=0)
            acc = acc + jnp.dot(weight.astype(jnp.bfloat16), pair, preferred_element_type=jnp.float32)
        os[j] = (acc / jnp.sum(total, axis=1, keepdims=True)).astype(jnp.bfloat16)

        @pl.when(i < 7)
        def _():
            remote(os.at[j], out.at[:, columns(head)], out_send.at[j], out_recv.at[g], (f, j))

        @pl.when(i == 7)
        def _():
            pltpu.make_async_copy(os.at[j], out.at[:, columns(head)], out_recv.at[g]).start()

        return carry

    lax.fori_loop(0, 8, attend, 0)

    for copy in started:
        copy.wait_send()
    for o, _ in others:
        pltpu.make_async_copy(os.at[o], os.at[o], out_send.at[o]).wait()
    for o, h in others + [(g, head)]:
        dst = out.at[:, columns(h)]
        pltpu.make_async_copy(dst, dst, out_recv.at[o]).wait()


def body(queries, key_vectors, value_vectors, tile_lists, live_slots):
    dma = pltpu.SemaphoreType.DMA
    hbm = pl.BlockSpec(memory_space=pltpu.HBM)
    bf16, i32 = jnp.bfloat16, jnp.int32
    return pl.pallas_call(
        kernel,
        out_shape=jax.ShapeDtypeStruct(queries.shape, queries.dtype),
        in_specs=[hbm] * 5,
        out_specs=hbm,
        scratch_shapes=[
            pltpu.VMEM((80, 2, TILE, DIM), bf16),
            pltpu.VMEM((8, TILE, DIM), bf16),
            pltpu.VMEM((8, TILE, DIM), bf16),
            pltpu.VMEM((SLOTS // 2, TILE, 2 * TILE), jnp.float32),
            pltpu.VMEM(tile_lists.shape, i32),
            pltpu.VMEM(live_slots.shape, i32),
            pltpu.SMEM((2,) + tile_lists.shape[1:], i32),
            pltpu.SMEM((2, live_slots.shape[1]), i32),
            dma((7, 3)),
            dma((8, 3)),
            dma((9, 2, SUBS)),
            dma((9, 2, SUBS)),
            dma((8,)),
            dma((8,)),
            dma((2,)),
            dma((2,)),
            dma((4,)),
            dma((4, 2)),
            dma((4, 2)),
            dma((4, 2, SUBS)),
            dma((4, 2, SUBS)),
            dma((5, 2, SUBS)),
            dma((5, 2, SUBS)),
        ],
        compiler_params=pltpu.CompilerParams(
            collective_id=0, has_side_effects=True, vmem_limit_bytes=63 << 20
        ),
    )(queries, key_vectors, value_vectors, tile_lists, live_slots)


def solution(mesh):
    placed = (
        P(("frame", "head"), None),
        P(("frame", "head"), None),
        P(("frame", "head"), None),
        P("head", "frame", None),
        P("head", "frame"),
    )
    return jax.shard_map(
        body, mesh=mesh, in_specs=placed, out_specs=P(("frame", "head"), None), check_vma=False
    )
```

```python
import math

import jax
import jax.numpy as jnp
from jax import lax
from jax.experimental import pallas as pl
from jax.experimental.pallas import tpu as pltpu
from jax.sharding import PartitionSpec as P

TILE = 128
DIM = 128
SLOTS = 20
COLS = 32
PERX = 8
SUBS = 2
PIECE = 4 // SUBS
MESH = pl.DeviceIdType.MESH

DN1, DN2, UP1, UP2, SB0, SBD1, SBU1, SBD2, SBU2 = range(9)


def kernel(
    q_in, k_in, v_in, lists_in, live_in, out,
    kv, qs, os, scores, list_land, live_land, lists, live,
    a2a_send, a2a_recv, win_send, win_recv, out_send, out_recv, meta_send, meta_recv, meta_local,
    far_send, far_recv, chain_send, chain_recv, sib_send, sib_recv,
):
    f, g = lax.axis_index("frame"), lax.axis_index("head")
    m, c = lax.div(f, 2), lax.rem(f, 2)
    x = lax.div(m, PERX)
    zh, y = lax.div(g, 4), lax.rem(g, 4)
    b = lax.rem(zh + x, 2)
    head = b * 4 + y

    def half_of(rel):
        return lax.rem(b + lax.div(lax.rem(m + rel + COLS, COLS), PERX), 2)

    def device(rel, core):
        return (lax.rem(m + rel + COLS, COLS) * 2 + core, half_of(rel) * 4 + y)

    up, down, sibling = device(1, c), device(-1, c), device(0, 1 - c)

    def owner(i):
        far = 1 - lax.div(i, 4)
        zh2 = lax.rem(zh + far, 2)
        y2 = lax.rem(y + lax.rem(i, 4) + (1 - far), 4)
        return zh2 * 4 + y2, lax.rem(zh2 + x, 2) * 4 + y2

    def fixed_owner(i):
        far = 1 - i // 4
        zh2 = lax.rem(zh + far, 2)
        y2 = lax.rem(y + i % 4 + (1 - far), 4)
        return zh2 * 4 + y2, lax.rem(zh2 + x, 2) * 4 + y2

    others = [fixed_owner(i) for i in range(7)]

    def across_to(rel, y2):
        column = lax.rem(m + rel + COLS, COLS)
        return (column * 2 + c, lax.rem(1 - b + lax.div(column, PERX), 2) * 4 + y2)

    rows = [lax.rem(y + i, 4) for i in range(4)]
    barrier = pltpu.get_barrier_semaphore()
    for target in (
        [(f, o) for o, _ in others[4:]]
        + [up, down, sibling]
        + [across_to(rel, y2) for rel in (-2, 2) for y2 in rows]
    ):
        pl.semaphore_signal(barrier, inc=1, device_id=target, device_id_type=MESH)
    pl.semaphore_wait(barrier, 14)

    started = []

    def remote(src, dst, send, recv, target):
        copy = pltpu.make_async_remote_copy(
            src_ref=src, dst_ref=dst, send_sem=send, recv_sem=recv, device_id=target, device_id_type=MESH
        )
        copy.start()
        return copy

    def columns(h):
        return pl.ds(pl.multiple_of(h * DIM, DIM), DIM)

    slot0 = 32 + c * 8
    ins = (k_in, v_in, q_in)

    def landing(t, j):
        return qs.at[j] if t == 2 else kv.at[slot0 + j, t]

    def exchange(i, t):
        o, h = others[i]
        started.append(
            remote(ins[t].at[:, columns(h)], landing(t, g), a2a_send.at[i, t], a2a_recv.at[g, t], (f, o))
        )

    def arrived(t, j):
        dst = landing(t, j)
        pltpu.make_async_copy(dst, dst, a2a_recv.at[j, t]).wait()

    for i, y2 in enumerate(rows):
        for t, rel in ((0, 2), (1, -2)):
            src = ins[t].at[:, columns((1 - b) * 4 + y2)]
            dst = kv.at[(rel + 2) * 16 + c * 8 + g, t]
            started.append(remote(src, dst, far_send.at[i, t], far_recv.at[y, t], across_to(-rel, y2)))
    for i in range(4, 7):
        exchange(i, 0)
        exchange(i, 1)
    for t in range(3):
        pltpu.make_async_copy(ins[t].at[:, columns(head)], landing(t, g), a2a_recv.at[g, t]).start()
    for i in range(4, 7):
        exchange(i, 2)

    across = (f, lax.rem(g + 4, 8))
    own_lists = pltpu.make_async_copy(lists_in.at[0], lists.at[0], meta_local.at[0])
    own_live = pltpu.make_async_copy(live_in, live.at[pl.ds(0, 1)], meta_local.at[1])
    own_lists.start()
    own_live.start()

    def first_tile(rel, o, s):
        return lax.rem(half_of(rel) + o, 2) * 4 + s * PIECE

    def tiles(rel, core, o, s):
        return pl.ds((rel + 2) * 16 + core * 8 + first_tile(rel, o, s), PIECE)

    def window_copy(kind, rel_src, rel_dst, o, s, target):
        src = tiles(rel_src, c, o, s)
        first = src.start - (rel_src + 2) * 16 + (rel_dst + 2) * 16
        return pltpu.make_async_remote_copy(
            src_ref=kv.at[src],
            dst_ref=kv.at[pl.ds(first, PIECE)],
            send_sem=win_send.at[kind, o, s],
            recv_sem=win_recv.at[kind, o, s],
            device_id=target,
            device_id_type=MESH,
        )

    def pass_on(kind, rel_src, rel_dst, o, s, target):
        copy = window_copy(kind, rel_src, rel_dst, o, s, target)
        copy.start()
        started.append(copy)

    def window_wait(kind, rel, core, o, s):
        dst = kv.at[tiles(rel, core, o, s)]
        pltpu.make_async_copy(dst, dst, win_recv.at[kind, o, s]).wait()

    def own(o, s):
        for p in range(PIECE):
            j = first_tile(0, o, s) + p
            arrived(0, j)
            arrived(1, j)
        pass_on(DN1, 0, -1, o, s, up)
        pass_on(UP1, 0, 1, o, s, down)
        pass_on(SB0, 0, 0, o, s, sibling)

    def then(o, s):
        window_wait(DN1, -1, c, o, s)
        pass_on(DN2, -1, -2, o, s, up)
        pass_on(SBD1, -1, -1, o, s, sibling)
        window_wait(UP1, 1, c, o, s)
        pass_on(UP2, 1, 2, o, s, down)
        pass_on(SBU1, 1, 1, o, s, sibling)

    def chain_tiles(rel, core, t, s, to):
        return kv.at[pl.ds((to + 2) * 16 + core * 8 + first_tile(rel, 1, s), PIECE), t]

    def chain(stage):
        for s in range(SUBS):
            for t, rel, step, target in ((0, 2 - stage, -1, up), (1, stage - 2, 1, down)):
                if stage == 0:
                    for e in range(PIECE):
                        dst = kv.at[(rel + 2) * 16 + c * 8 + first_tile(rel, 1, s) + e, t]
                        pltpu.make_async_copy(dst, dst, far_recv.at[s * PIECE + e, t]).wait()
                else:
                    dst = chain_tiles(rel, c, t, s, rel)
                    pltpu.make_async_copy(dst, dst, chain_recv.at[stage - 1, t, s]).wait()
                if stage < 4:
                    src, dst = chain_tiles(rel, c, t, s, rel), chain_tiles(rel, c, t, s, rel + step)
                    started.append(remote(src, dst, chain_send.at[stage, t, s], chain_recv.at[stage, t, s], target))
                if abs(rel) < 2:
                    share(stage, t, rel, s).start()
                else:
                    pl.when(c == (0 if rel == 2 else 1))(share(stage, t, rel, s).start)

    def share(stage, t, rel, s):
        src = chain_tiles(rel, c, t, s, rel)
        return pltpu.make_async_remote_copy(
            src_ref=src,
            dst_ref=src,
            send_sem=sib_send.at[stage, t, s],
            recv_sem=sib_recv.at[stage, t, s],
            device_id=sibling,
            device_id_type=MESH,
        )

    def shared(stage, t, rel, s):
        dst = chain_tiles(rel, 1 - c, t, s, rel)
        wait = pltpu.make_async_copy(dst, dst, sib_recv.at[stage, t, s]).wait
        if abs(rel) < 2:
            wait()
            share(stage, t, rel, s).wait_send()
        else:
            sender = c == (0 if rel == 2 else 1)
            pl.when(sender)(share(stage, t, rel, s).wait_send)
            pl.when(jnp.logical_not(sender))(wait)

    q_copies = [
        pltpu.make_async_remote_copy(
            src_ref=q_in.at[:, columns(h)],
            dst_ref=qs.at[g],
            send_sem=a2a_send.at[i, 2],
            recv_sem=a2a_recv.at[g, 2],
            device_id=(f, o),
            device_id_type=MESH,
        )
        for i, (o, h) in enumerate(others[:4])
    ]
    started.extend(q_copies)

    def q_far(*some):
        for i in some:
            q_copies[i].start()

    soon = lax.rem(m, PERX) < 3
    for s in range(SUBS):
        own(0, s)
    chain(0)
    for s in range(SUBS):
        then(0, s)
    chain(1)
    q_far(0)
    chain(2)
    q_far(1)
    started.append(remote(lists_in, list_land, meta_send.at[0], meta_recv.at[0], across))
    started.append(remote(live_in, live_land, meta_send.at[1], meta_recv.at[1], across))
    chain(3)
    q_far(2, 3)
    chain(4)

    for o in (0,):
        for s in range(SUBS):
            window_wait(DN2, -2, c, o, s)

            @pl.when(c == 1)
            def _():
                window_copy(SBD2, -2, -2, o, s, sibling).start()

            window_wait(UP2, 2, c, o, s)

            @pl.when(c == 0)
            def _():
                window_copy(SBU2, 2, 2, o, s, sibling).start()

    for o in (0,):
        for s in range(SUBS):
            for kind, rel in ((SB0, 0), (SBD1, -1), (SBU1, 1)):
                window_wait(kind, rel, 1 - c, o, s)

            @pl.when(c == 0)
            def _():
                window_wait(SBD2, -2, 1, o, s)
                window_copy(SBU2, 2, 2, o, s, sibling).wait_send()

            @pl.when(c == 1)
            def _():
                window_wait(SBU2, 2, 0, o, s)
                window_copy(SBD2, -2, -2, o, s, sibling).wait_send()

    for stage in range(5):
        for s in range(SUBS):
            shared(stage, 0, 2 - stage, s)
            shared(stage, 1, stage - 2, s)

    pltpu.make_async_copy(list_land, list_land, meta_recv.at[0]).wait()
    pltpu.make_async_copy(live_land, live_land, meta_recv.at[1]).wait()
    own_lists.wait()
    own_live.wait()
    crossed_lists = pltpu.make_async_copy(list_land.at[0], lists.at[1], meta_local.at[2])
    crossed_live = pltpu.make_async_copy(live_land, live.at[pl.ds(1, 1)], meta_local.at[3])
    crossed_lists.start()
    crossed_live.start()
    crossed_lists.wait()
    crossed_live.wait()

    odd = lax.rem(x, 2)
    base = (m - 2) * 16
    factor = math.log2(math.e) / math.sqrt(DIM)

    turn = jnp.where(lax.rem(m, PERX) >= 3, 4, 0)

    def attend(i, carry):
        i = lax.rem(i + turn, 8)
        j, _ = owner(i)
        arrived(2, j)
        query = qs[j]
        ids = [jnp.clip(lists[odd, j, s] - base, 0, 79) for s in range(SLOTS)]
        count = live[odd, j]
        peak = jnp.full((TILE, 2 * TILE), -jnp.inf, jnp.float32)
        for s in range(0, SLOTS, 2):
            pair = jnp.concatenate([kv[ids[s], 0], kv[ids[s + 1], 0]], axis=0)
            raw = lax.dot_general(query, pair, (((1,), (1,)), ((), ())), preferred_element_type=jnp.float32)
            scores[s // 2] = raw
            peak = jnp.maximum(peak, raw)
        top = jnp.max(peak, axis=1, keepdims=True) * factor
        total = jnp.zeros((TILE, 2 * TILE), jnp.float32)
        acc = jnp.zeros((TILE, DIM), jnp.float32)
        lane = lax.broadcasted_iota(jnp.int32, (1, 2 * TILE), 1)
        for s in range(0, SLOTS, 2):
            dead = jnp.where(s + lax.div(lane, TILE) < count, 0.0, jnp.inf)
            weight = jnp.exp2(scores[s // 2] * factor - (top + dead))
            total = total + weight
            pair = jnp.concatenate([kv[ids[s], 1], kv[ids[s + 1], 1]], axis=0)
            acc = acc + jnp.dot(weight.astype(jnp.bfloat16), pair, preferred_element_type=jnp.float32)
        os[j] = (acc / jnp.sum(total, axis=1, keepdims=True)).astype(jnp.bfloat16)

        @pl.when(i < 7)
        def _():
            remote(os.at[j], out.at[:, columns(head)], out_send.at[j], out_recv.at[g], (f, j))

        @pl.when(i == 7)
        def _():
            pltpu.make_async_copy(os.at[j], out.at[:, columns(head)], out_recv.at[g]).start()

        return carry

    lax.fori_loop(0, 8, attend, 0)

    for copy in started:
        copy.wait_send()
    for o, _ in others:
        pltpu.make_async_copy(os.at[o], os.at[o], out_send.at[o]).wait()
    for o, h in others + [(g, head)]:
        dst = out.at[:, columns(h)]
        pltpu.make_async_copy(dst, dst, out_recv.at[o]).wait()


def body(queries, key_vectors, value_vectors, tile_lists, live_slots):
    dma = pltpu.SemaphoreType.DMA
    hbm = pl.BlockSpec(memory_space=pltpu.HBM)
    bf16, i32 = jnp.bfloat16, jnp.int32
    return pl.pallas_call(
        kernel,
        out_shape=jax.ShapeDtypeStruct(queries.shape, queries.dtype),
        in_specs=[hbm] * 5,
        out_specs=hbm,
        scratch_shapes=[
            pltpu.VMEM((80, 2, TILE, DIM), bf16),
            pltpu.VMEM((8, TILE, DIM), bf16),
            pltpu.VMEM((8, TILE, DIM), bf16),
            pltpu.VMEM((SLOTS // 2, TILE, 2 * TILE), jnp.float32),
            pltpu.VMEM(tile_lists.shape, i32),
            pltpu.VMEM(live_slots.shape, i32),
            pltpu.SMEM((2,) + tile_lists.shape[1:], i32),
            pltpu.SMEM((2, live_slots.shape[1]), i32),
            dma((7, 3)),
            dma((8, 3)),
            dma((9, 2, SUBS)),
            dma((9, 2, SUBS)),
            dma((8,)),
            dma((8,)),
            dma((2,)),
            dma((2,)),
            dma((4,)),
            dma((4, 2)),
            dma((4, 2)),
            dma((4, 2, SUBS)),
            dma((4, 2, SUBS)),
            dma((5, 2, SUBS)),
            dma((5, 2, SUBS)),
        ],
        compiler_params=pltpu.CompilerParams(
            collective_id=0, has_side_effects=True, vmem_limit_bytes=63 << 20
        ),
    )(queries, key_vectors, value_vectors, tile_lists, live_slots)


def solution(mesh):
    placed = (
        P(("frame", "head"), None),
        P(("frame", "head"), None),
        P(("frame", "head"), None),
        P("head", "frame", None),
        P("head", "frame"),
    )
    return jax.shard_map(
        body, mesh=mesh, in_specs=placed, out_specs=P(("frame", "head"), None), check_vma=False
    )
```

```python
import math

import jax
import jax.numpy as jnp
from jax import lax
from jax.experimental import pallas as pl
from jax.experimental.pallas import tpu as pltpu
from jax.sharding import PartitionSpec as P

TILE = 128
DIM = 128
SLOTS = 20
COLS = 32
PERX = 8
SUBS = 2
PIECE = 4 // SUBS
MESH = pl.DeviceIdType.MESH

DN1, DN2, UP1, UP2, SB0, SBD1, SBU1, SBD2, SBU2 = range(9)


def kernel(
    q_in, k_in, v_in, lists_in, live_in, out,
    kv, qs, os, scores, list_land, live_land, lists, live,
    a2a_send, a2a_recv, win_send, win_recv, out_send, out_recv, meta_send, meta_recv, meta_local,
    far_send, far_recv, chain_send, chain_recv, sib_send, sib_recv,
):
    f, g = lax.axis_index("frame"), lax.axis_index("head")
    m, c = lax.div(f, 2), lax.rem(f, 2)
    x = lax.div(m, PERX)
    zh, y = lax.div(g, 4), lax.rem(g, 4)
    b = lax.rem(zh + x, 2)
    head = b * 4 + y

    def half_of(rel):
        return lax.rem(b + lax.div(lax.rem(m + rel + COLS, COLS), PERX), 2)

    def device(rel, core):
        return (lax.rem(m + rel + COLS, COLS) * 2 + core, half_of(rel) * 4 + y)

    up, down, sibling = device(1, c), device(-1, c), device(0, 1 - c)

    def owner(i):
        far = 1 - lax.div(i, 4)
        zh2 = lax.rem(zh + far, 2)
        y2 = lax.rem(y + lax.rem(i, 4) + (1 - far), 4)
        return zh2 * 4 + y2, lax.rem(zh2 + x, 2) * 4 + y2

    def fixed_owner(i):
        far = 1 - i // 4
        zh2 = lax.rem(zh + far, 2)
        y2 = lax.rem(y + i % 4 + (1 - far), 4)
        return zh2 * 4 + y2, lax.rem(zh2 + x, 2) * 4 + y2

    others = [fixed_owner(i) for i in range(7)]

    def across_to(rel, y2):
        column = lax.rem(m + rel + COLS, COLS)
        return (column * 2 + c, lax.rem(1 - b + lax.div(column, PERX), 2) * 4 + y2)

    rows = [lax.rem(y + i, 4) for i in range(4)]
    barrier = pltpu.get_barrier_semaphore()
    for target in (
        [(f, o) for o, _ in others[4:]]
        + [up, down, sibling]
        + [across_to(rel, y2) for rel in (-2, 2) for y2 in rows]
    ):
        pl.semaphore_signal(barrier, inc=1, device_id=target, device_id_type=MESH)
    pl.semaphore_wait(barrier, 14)

    started = []

    def remote(src, dst, send, recv, target):
        copy = pltpu.make_async_remote_copy(
            src_ref=src, dst_ref=dst, send_sem=send, recv_sem=recv, device_id=target, device_id_type=MESH
        )
        copy.start()
        return copy

    def columns(h):
        return pl.ds(pl.multiple_of(h * DIM, DIM), DIM)

    slot0 = 32 + c * 8
    ins = (k_in, v_in, q_in)

    def landing(t, j):
        return qs.at[j] if t == 2 else kv.at[slot0 + j, t]

    def exchange(i, t):
        o, h = others[i]
        started.append(
            remote(ins[t].at[:, columns(h)], landing(t, g), a2a_send.at[i, t], a2a_recv.at[g, t], (f, o))
        )

    def arrived(t, j):
        dst = landing(t, j)
        pltpu.make_async_copy(dst, dst, a2a_recv.at[j, t]).wait()

    for i, y2 in enumerate(rows):
        for t, rel in ((0, 2), (1, -2)):
            src = ins[t].at[:, columns((1 - b) * 4 + y2)]
            dst = kv.at[(rel + 2) * 16 + c * 8 + g, t]
            started.append(remote(src, dst, far_send.at[i, t], far_recv.at[y, t], across_to(-rel, y2)))
    for i in range(4, 7):
        exchange(i, 0)
        exchange(i, 1)
    for t in range(3):
        pltpu.make_async_copy(ins[t].at[:, columns(head)], landing(t, g), a2a_recv.at[g, t]).start()
    for i in range(4, 7):
        exchange(i, 2)

    across = (f, lax.rem(g + 4, 8))
    own_lists = pltpu.make_async_copy(lists_in.at[0], lists.at[0], meta_local.at[0])
    own_live = pltpu.make_async_copy(live_in, live.at[pl.ds(0, 1)], meta_local.at[1])
    own_lists.start()
    own_live.start()

    def first_tile(rel, o, s):
        return lax.rem(half_of(rel) + o, 2) * 4 + s * PIECE

    def tiles(rel, core, o, s):
        return pl.ds((rel + 2) * 16 + core * 8 + first_tile(rel, o, s), PIECE)

    def window_copy(kind, rel_src, rel_dst, o, s, target):
        src = tiles(rel_src, c, o, s)
        first = src.start - (rel_src + 2) * 16 + (rel_dst + 2) * 16
        return pltpu.make_async_remote_copy(
            src_ref=kv.at[src],
            dst_ref=kv.at[pl.ds(first, PIECE)],
            send_sem=win_send.at[kind, o, s],
            recv_sem=win_recv.at[kind, o, s],
            device_id=target,
            device_id_type=MESH,
        )

    def pass_on(kind, rel_src, rel_dst, o, s, target):
        copy = window_copy(kind, rel_src, rel_dst, o, s, target)
        copy.start()
        started.append(copy)

    def window_wait(kind, rel, core, o, s):
        dst = kv.at[tiles(rel, core, o, s)]
        pltpu.make_async_copy(dst, dst, win_recv.at[kind, o, s]).wait()

    def own(o, s):
        for p in range(PIECE):
            j = first_tile(0, o, s) + p
            arrived(0, j)
            arrived(1, j)
        pass_on(DN1, 0, -1, o, s, up)
        pass_on(UP1, 0, 1, o, s, down)
        pass_on(SB0, 0, 0, o, s, sibling)

    def then(o, s):
        window_wait(DN1, -1, c, o, s)
        pass_on(DN2, -1, -2, o, s, up)
        pass_on(SBD1, -1, -1, o, s, sibling)
        window_wait(UP1, 1, c, o, s)
        pass_on(UP2, 1, 2, o, s, down)
        pass_on(SBU1, 1, 1, o, s, sibling)

    def chain_tiles(rel, core, t, s, to):
        return kv.at[pl.ds((to + 2) * 16 + core * 8 + first_tile(rel, 1, s), PIECE), t]

    def chain(stage):
        for s in range(SUBS):
            for t, rel, step, target in ((0, 2 - stage, -1, up), (1, stage - 2, 1, down)):
                if stage == 0:
                    for e in range(PIECE):
                        dst = kv.at[(rel + 2) * 16 + c * 8 + first_tile(rel, 1, s) + e, t]
                        pltpu.make_async_copy(dst, dst, far_recv.at[s * PIECE + e, t]).wait()
                else:
                    dst = chain_tiles(rel, c, t, s, rel)
                    pltpu.make_async_copy(dst, dst, chain_recv.at[stage - 1, t, s]).wait()
                if stage < 4:
                    src, dst = chain_tiles(rel, c, t, s, rel), chain_tiles(rel, c, t, s, rel + step)
                    started.append(remote(src, dst, chain_send.at[stage, t, s], chain_recv.at[stage, t, s], target))
                if abs(rel) < 2:
                    share(stage, t, rel, s).start()
                else:
                    pl.when(c == (0 if rel == 2 else 1))(share(stage, t, rel, s).start)

    def share(stage, t, rel, s):
        src = chain_tiles(rel, c, t, s, rel)
        return pltpu.make_async_remote_copy(
            src_ref=src,
            dst_ref=src,
            send_sem=sib_send.at[stage, t, s],
            recv_sem=sib_recv.at[stage, t, s],
            device_id=sibling,
            device_id_type=MESH,
        )

    def shared(stage, t, rel, s):
        dst = chain_tiles(rel, 1 - c, t, s, rel)
        wait = pltpu.make_async_copy(dst, dst, sib_recv.at[stage, t, s]).wait
        if abs(rel) < 2:
            wait()
            share(stage, t, rel, s).wait_send()
        else:
            sender = c == (0 if rel == 2 else 1)
            pl.when(sender)(share(stage, t, rel, s).wait_send)
            pl.when(jnp.logical_not(sender))(wait)

    q_copies = [
        pltpu.make_async_remote_copy(
            src_ref=q_in.at[:, columns(h)],
            dst_ref=qs.at[g],
            send_sem=a2a_send.at[i, 2],
            recv_sem=a2a_recv.at[g, 2],
            device_id=(f, o),
            device_id_type=MESH,
        )
        for i, (o, h) in enumerate(others[:4])
    ]
    started.extend(q_copies)

    def q_far(*some):
        for i in some:
            q_copies[i].start()

    for s in range(SUBS):
        own(0, s)
    chain(0)
    for s in range(SUBS):
        then(0, s)
    chain(1)
    q_far(0)
    chain(2)
    q_far(1)
    started.append(remote(lists_in, list_land, meta_send.at[0], meta_recv.at[0], across))
    started.append(remote(live_in, live_land, meta_send.at[1], meta_recv.at[1], across))
    chain(3)
    q_far(2, 3)
    chain(4)

    for o in (0,):
        for s in range(SUBS):
            window_wait(DN2, -2, c, o, s)

            @pl.when(c == 1)
            def _():
                window_copy(SBD2, -2, -2, o, s, sibling).start()

            window_wait(UP2, 2, c, o, s)

            @pl.when(c == 0)
            def _():
                window_copy(SBU2, 2, 2, o, s, sibling).start()

    for o in (0,):
        for s in range(SUBS):
            for kind, rel in ((SB0, 0), (SBD1, -1), (SBU1, 1)):
                window_wait(kind, rel, 1 - c, o, s)

            @pl.when(c == 0)
            def _():
                window_wait(SBD2, -2, 1, o, s)
                window_copy(SBU2, 2, 2, o, s, sibling).wait_send()

            @pl.when(c == 1)
            def _():
                window_wait(SBU2, 2, 0, o, s)
                window_copy(SBD2, -2, -2, o, s, sibling).wait_send()

    for stage in range(5):
        for s in range(SUBS):
            shared(stage, 0, 2 - stage, s)
            shared(stage, 1, stage - 2, s)

    pltpu.make_async_copy(list_land, list_land, meta_recv.at[0]).wait()
    pltpu.make_async_copy(live_land, live_land, meta_recv.at[1]).wait()
    own_lists.wait()
    own_live.wait()
    crossed_lists = pltpu.make_async_copy(list_land.at[0], lists.at[1], meta_local.at[2])
    crossed_live = pltpu.make_async_copy(live_land, live.at[pl.ds(1, 1)], meta_local.at[3])
    crossed_lists.start()
    crossed_live.start()
    crossed_lists.wait()
    crossed_live.wait()

    odd = lax.rem(x, 2)
    base = (m - 2) * 16
    factor = math.log2(math.e) / math.sqrt(DIM)

    def attend(i, carry):
        j, _ = owner(i)
        arrived(2, j)
        query = qs[j]
        ids = [jnp.clip(lists[odd, j, s] - base, 0, 79) for s in range(SLOTS)]
        count = live[odd, j]
        peak = jnp.full((TILE, 2 * TILE), -jnp.inf, jnp.float32)
        for s in range(0, SLOTS, 2):
            pair = jnp.concatenate([kv[ids[s], 0], kv[ids[s + 1], 0]], axis=0)
            raw = lax.dot_general(query, pair, (((1,), (1,)), ((), ())), preferred_element_type=jnp.float32)
            scores[s // 2] = raw
            peak = jnp.maximum(peak, raw)
        top = jnp.max(peak, axis=1, keepdims=True) * factor
        total = jnp.zeros((TILE, 2 * TILE), jnp.float32)
        acc = jnp.zeros((TILE, DIM), jnp.float32)
        lane = lax.broadcasted_iota(jnp.int32, (1, 2 * TILE), 1)
        for s in range(0, SLOTS, 2):
            dead = jnp.where(s + lax.div(lane, TILE) < count, 0.0, jnp.inf)
            weight = jnp.exp2(scores[s // 2] * factor - (top + dead))
            total = total + weight
            pair = jnp.concatenate([kv[ids[s], 1], kv[ids[s + 1], 1]], axis=0)
            acc = acc + jnp.dot(weight.astype(jnp.bfloat16), pair, preferred_element_type=jnp.float32)
        os[j] = (acc / jnp.sum(total, axis=1, keepdims=True)).astype(jnp.bfloat16)

        @pl.when(i < 7)
        def _():
            remote(os.at[j], out.at[:, columns(head)], out_send.at[j], out_recv.at[g], (f, j))

        @pl.when(i == 7)
        def _():
            pltpu.make_async_copy(os.at[j], out.at[:, columns(head)], out_recv.at[g]).start()

        return carry

    lax.fori_loop(0, 8, attend, 0)

    for copy in started:
        copy.wait_send()
    for o, _ in others:
        pltpu.make_async_copy(os.at[o], os.at[o], out_send.at[o]).wait()
    for o, h in others + [(g, head)]:
        dst = out.at[:, columns(h)]
        pltpu.make_async_copy(dst, dst, out_recv.at[o]).wait()


def body(queries, key_vectors, value_vectors, tile_lists, live_slots):
    dma = pltpu.SemaphoreType.DMA
    hbm = pl.BlockSpec(memory_space=pltpu.HBM)
    bf16, i32 = jnp.bfloat16, jnp.int32
    return pl.pallas_call(
        kernel,
        out_shape=jax.ShapeDtypeStruct(queries.shape, queries.dtype),
        in_specs=[hbm] * 5,
        out_specs=hbm,
        scratch_shapes=[
            pltpu.VMEM((80, 2, TILE, DIM), bf16),
            pltpu.VMEM((8, TILE, DIM), bf16),
            pltpu.VMEM((8, TILE, DIM), bf16),
            pltpu.VMEM((SLOTS // 2, TILE, 2 * TILE), jnp.float32),
            pltpu.VMEM(tile_lists.shape, i32),
            pltpu.VMEM(live_slots.shape, i32),
            pltpu.SMEM((2,) + tile_lists.shape[1:], i32),
            pltpu.SMEM((2, live_slots.shape[1]), i32),
            dma((7, 3)),
            dma((8, 3)),
            dma((9, 2, SUBS)),
            dma((9, 2, SUBS)),
            dma((8,)),
            dma((8,)),
            dma((2,)),
            dma((2,)),
            dma((4,)),
            dma((4, 2)),
            dma((4, 2)),
            dma((4, 2, SUBS)),
            dma((4, 2, SUBS)),
            dma((5, 2, SUBS)),
            dma((5, 2, SUBS)),
        ],
        compiler_params=pltpu.CompilerParams(
            collective_id=0, has_side_effects=True, vmem_limit_bytes=63 << 20
        ),
    )(queries, key_vectors, value_vectors, tile_lists, live_slots)


def solution(mesh):
    placed = (
        P(("frame", "head"), None),
        P(("frame", "head"), None),
        P(("frame", "head"), None),
        P("head", "frame", None),
        P("head", "frame"),
    )
    return jax.shard_map(
        body, mesh=mesh, in_specs=placed, out_specs=P(("frame", "head"), None), check_vma=False
    )
```

```python
import math

import jax
import jax.numpy as jnp
from jax import lax
from jax.experimental import pallas as pl
from jax.experimental.pallas import tpu as pltpu
from jax.sharding import PartitionSpec as P

TILE = 128
DIM = 128
SLOTS = 20
COLS = 32
PERX = 8
SUBS = 2
PIECE = 4 // SUBS
MESH = pl.DeviceIdType.MESH

DN1, DN2, UP1, UP2, SB0, SBD1, SBU1, SBD2, SBU2 = range(9)


def kernel(
    q_in, k_in, v_in, lists_in, live_in, out,
    kv, qs, os, scores, list_land, live_land, lists, live,
    a2a_send, a2a_recv, win_send, win_recv, out_send, out_recv, meta_send, meta_recv, meta_local,
    far_send, far_recv, chain_send, chain_recv, sib_send, sib_recv,
):
    f, g = lax.axis_index("frame"), lax.axis_index("head")
    m, c = lax.div(f, 2), lax.rem(f, 2)
    x = lax.div(m, PERX)
    zh, y = lax.div(g, 4), lax.rem(g, 4)
    b = lax.rem(zh + x, 2)
    head = b * 4 + y

    def half_of(rel):
        return lax.rem(b + lax.div(lax.rem(m + rel + COLS, COLS), PERX), 2)

    def device(rel, core):
        return (lax.rem(m + rel + COLS, COLS) * 2 + core, half_of(rel) * 4 + y)

    up, down, sibling = device(1, c), device(-1, c), device(0, 1 - c)

    def owner(i):
        far = 1 - lax.div(i, 4)
        zh2 = lax.rem(zh + far, 2)
        y2 = lax.rem(y + lax.rem(i, 4) + (1 - far), 4)
        return zh2 * 4 + y2, lax.rem(zh2 + x, 2) * 4 + y2

    def fixed_owner(i):
        far = 1 - i // 4
        zh2 = lax.rem(zh + far, 2)
        y2 = lax.rem(y + i % 4 + (1 - far), 4)
        return zh2 * 4 + y2, lax.rem(zh2 + x, 2) * 4 + y2

    others = [fixed_owner(i) for i in range(7)]

    def across_to(rel, y2):
        column = lax.rem(m + rel + COLS, COLS)
        return (column * 2 + c, lax.rem(1 - b + lax.div(column, PERX), 2) * 4 + y2)

    rows = [lax.rem(y + i, 4) for i in range(4)]
    barrier = pltpu.get_barrier_semaphore()
    for target in (
        [(f, o) for o, _ in others[4:]]
        + [up, down, sibling]
        + [across_to(rel, y2) for rel in (-2, 2) for y2 in rows]
    ):
        pl.semaphore_signal(barrier, inc=1, device_id=target, device_id_type=MESH)
    pl.semaphore_wait(barrier, 14)

    started = []

    def remote(src, dst, send, recv, target):
        copy = pltpu.make_async_remote_copy(
            src_ref=src, dst_ref=dst, send_sem=send, recv_sem=recv, device_id=target, device_id_type=MESH
        )
        copy.start()
        return copy

    def columns(h):
        return pl.ds(pl.multiple_of(h * DIM, DIM), DIM)

    slot0 = 32 + c * 8
    ins = (k_in, v_in, q_in)

    def landing(t, j):
        return qs.at[j] if t == 2 else kv.at[slot0 + j, t]

    def exchange(i, t):
        o, h = others[i]
        started.append(
            remote(ins[t].at[:, columns(h)], landing(t, g), a2a_send.at[i, t], a2a_recv.at[g, t], (f, o))
        )

    def arrived(t, j):
        dst = landing(t, j)
        pltpu.make_async_copy(dst, dst, a2a_recv.at[j, t]).wait()

    for i, y2 in enumerate(rows):
        for t, rel in ((0, 2), (1, -2)):
            src = ins[t].at[:, columns((1 - b) * 4 + y2)]
            dst = kv.at[(rel + 2) * 16 + c * 8 + g, t]
            started.append(remote(src, dst, far_send.at[i, t], far_recv.at[y, t], across_to(-rel, y2)))
    for i in range(4, 7):
        exchange(i, 0)
        exchange(i, 1)
    for t in range(3):
        pltpu.make_async_copy(ins[t].at[:, columns(head)], landing(t, g), a2a_recv.at[g, t]).start()
    for i in range(4, 7):
        exchange(i, 2)

    across = (f, lax.rem(g + 4, 8))
    own_lists = pltpu.make_async_copy(lists_in.at[0], lists.at[0], meta_local.at[0])
    own_live = pltpu.make_async_copy(live_in, live.at[pl.ds(0, 1)], meta_local.at[1])
    own_lists.start()
    own_live.start()

    def first_tile(rel, o, s):
        return lax.rem(half_of(rel) + o, 2) * 4 + s * PIECE

    def tiles(rel, core, o, s):
        return pl.ds((rel + 2) * 16 + core * 8 + first_tile(rel, o, s), PIECE)

    def window_copy(kind, rel_src, rel_dst, o, s, target):
        src = tiles(rel_src, c, o, s)
        first = src.start - (rel_src + 2) * 16 + (rel_dst + 2) * 16
        return pltpu.make_async_remote_copy(
            src_ref=kv.at[src],
            dst_ref=kv.at[pl.ds(first, PIECE)],
            send_sem=win_send.at[kind, o, s],
            recv_sem=win_recv.at[kind, o, s],
            device_id=target,
            device_id_type=MESH,
        )

    def pass_on(kind, rel_src, rel_dst, o, s, target):
        copy = window_copy(kind, rel_src, rel_dst, o, s, target)
        copy.start()
        started.append(copy)

    def window_wait(kind, rel, core, o, s):
        dst = kv.at[tiles(rel, core, o, s)]
        pltpu.make_async_copy(dst, dst, win_recv.at[kind, o, s]).wait()

    def own(o, s):
        for p in range(PIECE):
            j = first_tile(0, o, s) + p
            arrived(0, j)
            arrived(1, j)
        pass_on(DN1, 0, -1, o, s, up)
        pass_on(UP1, 0, 1, o, s, down)
        pass_on(SB0, 0, 0, o, s, sibling)

    def then(o, s):
        window_wait(DN1, -1, c, o, s)
        pass_on(DN2, -1, -2, o, s, up)
        pass_on(SBD1, -1, -1, o, s, sibling)
        window_wait(UP1, 1, c, o, s)
        pass_on(UP2, 1, 2, o, s, down)
        pass_on(SBU1, 1, 1, o, s, sibling)

    def chain_tiles(rel, core, t, s, to):
        return kv.at[pl.ds((to + 2) * 16 + core * 8 + first_tile(rel, 1, s), PIECE), t]

    def chain(stage):
        for s in range(SUBS):
            for t, rel, step, target in ((0, 2 - stage, -1, up), (1, stage - 2, 1, down)):
                if stage == 0:
                    for e in range(PIECE):
                        dst = kv.at[(rel + 2) * 16 + c * 8 + first_tile(rel, 1, s) + e, t]
                        pltpu.make_async_copy(dst, dst, far_recv.at[s * PIECE + e, t]).wait()
                else:
                    dst = chain_tiles(rel, c, t, s, rel)
                    pltpu.make_async_copy(dst, dst, chain_recv.at[stage - 1, t, s]).wait()
                if stage < 4:
                    src, dst = chain_tiles(rel, c, t, s, rel), chain_tiles(rel, c, t, s, rel + step)
                    started.append(remote(src, dst, chain_send.at[stage, t, s], chain_recv.at[stage, t, s], target))
                if abs(rel) < 2:
                    share(stage, t, rel, s).start()
                else:
                    pl.when(c == (0 if rel == 2 else 1))(share(stage, t, rel, s).start)

    def share(stage, t, rel, s):
        src = chain_tiles(rel, c, t, s, rel)
        return pltpu.make_async_remote_copy(
            src_ref=src,
            dst_ref=src,
            send_sem=sib_send.at[stage, t, s],
            recv_sem=sib_recv.at[stage, t, s],
            device_id=sibling,
            device_id_type=MESH,
        )

    def shared(stage, t, rel, s):
        dst = chain_tiles(rel, 1 - c, t, s, rel)
        wait = pltpu.make_async_copy(dst, dst, sib_recv.at[stage, t, s]).wait
        if abs(rel) < 2:
            wait()
            share(stage, t, rel, s).wait_send()
        else:
            sender = c == (0 if rel == 2 else 1)
            pl.when(sender)(share(stage, t, rel, s).wait_send)
            pl.when(jnp.logical_not(sender))(wait)

    q_copies = [
        pltpu.make_async_remote_copy(
            src_ref=q_in.at[:, columns(h)],
            dst_ref=qs.at[g],
            send_sem=a2a_send.at[i, 2],
            recv_sem=a2a_recv.at[g, 2],
            device_id=(f, o),
            device_id_type=MESH,
        )
        for i, (o, h) in enumerate(others[:4])
    ]
    started.extend(q_copies)

    def q_far(*some):
        for i in some:
            q_copies[i].start()

    for s in range(SUBS):
        own(0, s)
    chain(0)
    for s in range(SUBS):
        then(0, s)
    chain(1)
    q_far(0, 1)
    chain(2)
    q_far(2)
    started.append(remote(lists_in, list_land, meta_send.at[0], meta_recv.at[0], across))
    started.append(remote(live_in, live_land, meta_send.at[1], meta_recv.at[1], across))
    chain(3)
    q_far(3)
    chain(4)

    for o in (0,):
        for s in range(SUBS):
            window_wait(DN2, -2, c, o, s)

            @pl.when(c == 1)
            def _():
                window_copy(SBD2, -2, -2, o, s, sibling).start()

            window_wait(UP2, 2, c, o, s)

            @pl.when(c == 0)
            def _():
                window_copy(SBU2, 2, 2, o, s, sibling).start()

    for o in (0,):
        for s in range(SUBS):
            for kind, rel in ((SB0, 0), (SBD1, -1), (SBU1, 1)):
                window_wait(kind, rel, 1 - c, o, s)

            @pl.when(c == 0)
            def _():
                window_wait(SBD2, -2, 1, o, s)
                window_copy(SBU2, 2, 2, o, s, sibling).wait_send()

            @pl.when(c == 1)
            def _():
                window_wait(SBU2, 2, 0, o, s)
                window_copy(SBD2, -2, -2, o, s, sibling).wait_send()

    for stage in range(5):
        for s in range(SUBS):
            shared(stage, 0, 2 - stage, s)
            shared(stage, 1, stage - 2, s)

    pltpu.make_async_copy(list_land, list_land, meta_recv.at[0]).wait()
    pltpu.make_async_copy(live_land, live_land, meta_recv.at[1]).wait()
    own_lists.wait()
    own_live.wait()
    crossed_lists = pltpu.make_async_copy(list_land.at[0], lists.at[1], meta_local.at[2])
    crossed_live = pltpu.make_async_copy(live_land, live.at[pl.ds(1, 1)], meta_local.at[3])
    crossed_lists.start()
    crossed_live.start()
    crossed_lists.wait()
    crossed_live.wait()

    odd = lax.rem(x, 2)
    base = (m - 2) * 16
    factor = math.log2(math.e) / math.sqrt(DIM)

    def attend(i, carry):
        j, _ = owner(i)
        arrived(2, j)
        query = qs[j]
        ids = [jnp.clip(lists[odd, j, s] - base, 0, 79) for s in range(SLOTS)]
        count = live[odd, j]
        peak = jnp.full((TILE, 2 * TILE), -jnp.inf, jnp.float32)
        for s in range(0, SLOTS, 2):
            pair = jnp.concatenate([kv[ids[s], 0], kv[ids[s + 1], 0]], axis=0)
            raw = lax.dot_general(query, pair, (((1,), (1,)), ((), ())), preferred_element_type=jnp.float32)
            scores[s // 2] = raw
            peak = jnp.maximum(peak, raw)
        top = jnp.max(peak, axis=1, keepdims=True) * factor
        total = jnp.zeros((TILE, 2 * TILE), jnp.float32)
        acc = jnp.zeros((TILE, DIM), jnp.float32)
        lane = lax.broadcasted_iota(jnp.int32, (1, 2 * TILE), 1)
        for s in range(0, SLOTS, 2):
            dead = jnp.where(s + lax.div(lane, TILE) < count, 0.0, jnp.inf)
            weight = jnp.exp2(scores[s // 2] * factor - (top + dead))
            total = total + weight
            pair = jnp.concatenate([kv[ids[s], 1], kv[ids[s + 1], 1]], axis=0)
            acc = acc + jnp.dot(weight.astype(jnp.bfloat16), pair, preferred_element_type=jnp.float32)
        os[j] = (acc / jnp.sum(total, axis=1, keepdims=True)).astype(jnp.bfloat16)

        @pl.when(i < 7)
        def _():
            remote(os.at[j], out.at[:, columns(head)], out_send.at[j], out_recv.at[g], (f, j))

        @pl.when(i == 7)
        def _():
            pltpu.make_async_copy(os.at[j], out.at[:, columns(head)], out_recv.at[g]).start()

        return carry

    lax.fori_loop(0, 8, attend, 0)

    for copy in started:
        copy.wait_send()
    for o, _ in others:
        pltpu.make_async_copy(os.at[o], os.at[o], out_send.at[o]).wait()
    for o, h in others + [(g, head)]:
        dst = out.at[:, columns(h)]
        pltpu.make_async_copy(dst, dst, out_recv.at[o]).wait()


def body(queries, key_vectors, value_vectors, tile_lists, live_slots):
    dma = pltpu.SemaphoreType.DMA
    hbm = pl.BlockSpec(memory_space=pltpu.HBM)
    bf16, i32 = jnp.bfloat16, jnp.int32
    return pl.pallas_call(
        kernel,
        out_shape=jax.ShapeDtypeStruct(queries.shape, queries.dtype),
        in_specs=[hbm] * 5,
        out_specs=hbm,
        scratch_shapes=[
            pltpu.VMEM((80, 2, TILE, DIM), bf16),
            pltpu.VMEM((8, TILE, DIM), bf16),
            pltpu.VMEM((8, TILE, DIM), bf16),
            pltpu.VMEM((SLOTS // 2, TILE, 2 * TILE), jnp.float32),
            pltpu.VMEM(tile_lists.shape, i32),
            pltpu.VMEM(live_slots.shape, i32),
            pltpu.SMEM((2,) + tile_lists.shape[1:], i32),
            pltpu.SMEM((2, live_slots.shape[1]), i32),
            dma((7, 3)),
            dma((8, 3)),
            dma((9, 2, SUBS)),
            dma((9, 2, SUBS)),
            dma((8,)),
            dma((8,)),
            dma((2,)),
            dma((2,)),
            dma((4,)),
            dma((4, 2)),
            dma((4, 2)),
            dma((4, 2, SUBS)),
            dma((4, 2, SUBS)),
            dma((5, 2, SUBS)),
            dma((5, 2, SUBS)),
        ],
        compiler_params=pltpu.CompilerParams(
            collective_id=0, has_side_effects=True, vmem_limit_bytes=63 << 20
        ),
    )(queries, key_vectors, value_vectors, tile_lists, live_slots)


def solution(mesh):
    placed = (
        P(("frame", "head"), None),
        P(("frame", "head"), None),
        P(("frame", "head"), None),
        P("head", "frame", None),
        P("head", "frame"),
    )
    return jax.shard_map(
        body, mesh=mesh, in_specs=placed, out_specs=P(("frame", "head"), None), check_vma=False
    )
```

```python
import math

import jax
import jax.numpy as jnp
from jax import lax
from jax.experimental import pallas as pl
from jax.experimental.pallas import tpu as pltpu
from jax.sharding import PartitionSpec as P

TILE = 128
DIM = 128
SLOTS = 20
COLS = 32
PERX = 8
SUBS = 2
PIECE = 4 // SUBS
MESH = pl.DeviceIdType.MESH

DN1, DN2, UP1, UP2, SB0, SBD1, SBU1, SBD2, SBU2 = range(9)


def kernel(
    q_in, k_in, v_in, lists_in, live_in, out,
    kv, qs, os, scores, list_land, live_land, lists, live,
    a2a_send, a2a_recv, win_send, win_recv, out_send, out_recv, meta_send, meta_recv, meta_local,
    far_send, far_recv, chain_send, chain_recv, sib_send, sib_recv,
):
    f, g = lax.axis_index("frame"), lax.axis_index("head")
    m, c = lax.div(f, 2), lax.rem(f, 2)
    x = lax.div(m, PERX)
    zh, y = lax.div(g, 4), lax.rem(g, 4)
    b = lax.rem(zh + x, 2)
    head = b * 4 + y

    def half_of(rel):
        return lax.rem(b + lax.div(lax.rem(m + rel + COLS, COLS), PERX), 2)

    def device(rel, core):
        return (lax.rem(m + rel + COLS, COLS) * 2 + core, half_of(rel) * 4 + y)

    up, down, sibling = device(1, c), device(-1, c), device(0, 1 - c)

    def owner(i):
        far = 1 - lax.div(i, 4)
        zh2 = lax.rem(zh + far, 2)
        y2 = lax.rem(y + lax.rem(i, 4) + (1 - far), 4)
        return zh2 * 4 + y2, lax.rem(zh2 + x, 2) * 4 + y2

    def fixed_owner(i):
        far = 1 - i // 4
        zh2 = lax.rem(zh + far, 2)
        y2 = lax.rem(y + i % 4 + (1 - far), 4)
        return zh2 * 4 + y2, lax.rem(zh2 + x, 2) * 4 + y2

    others = [fixed_owner(i) for i in range(7)]

    def across_to(rel, y2):
        column = lax.rem(m + rel + COLS, COLS)
        return (column * 2 + c, lax.rem(1 - b + lax.div(column, PERX), 2) * 4 + y2)

    rows = [lax.rem(y + i, 4) for i in range(4)]
    barrier = pltpu.get_barrier_semaphore()
    for target in (
        [(f, o) for o, _ in others[4:]]
        + [up, down, sibling]
        + [across_to(rel, y2) for rel in (-2, 2) for y2 in rows]
    ):
        pl.semaphore_signal(barrier, inc=1, device_id=target, device_id_type=MESH)
    pl.semaphore_wait(barrier, 14)

    started = []

    def remote(src, dst, send, recv, target):
        copy = pltpu.make_async_remote_copy(
            src_ref=src, dst_ref=dst, send_sem=send, recv_sem=recv, device_id=target, device_id_type=MESH
        )
        copy.start()
        return copy

    def columns(h):
        return pl.ds(pl.multiple_of(h * DIM, DIM), DIM)

    slot0 = 32 + c * 8
    ins = (k_in, v_in, q_in)

    def landing(t, j):
        return qs.at[j] if t == 2 else kv.at[slot0 + j, t]

    def exchange(i, t):
        o, h = others[i]
        started.append(
            remote(ins[t].at[:, columns(h)], landing(t, g), a2a_send.at[i, t], a2a_recv.at[g, t], (f, o))
        )

    def arrived(t, j):
        dst = landing(t, j)
        pltpu.make_async_copy(dst, dst, a2a_recv.at[j, t]).wait()

    for i, y2 in enumerate(rows):
        for t, rel in ((0, 2), (1, -2)):
            src = ins[t].at[:, columns((1 - b) * 4 + y2)]
            dst = kv.at[(rel + 2) * 16 + c * 8 + g, t]
            started.append(remote(src, dst, far_send.at[i, t], far_recv.at[y, t], across_to(-rel, y2)))
    for i in range(4, 7):
        exchange(i, 0)
        exchange(i, 1)
    for t in range(3):
        pltpu.make_async_copy(ins[t].at[:, columns(head)], landing(t, g), a2a_recv.at[g, t]).start()

    across = (f, lax.rem(g + 4, 8))
    own_lists = pltpu.make_async_copy(lists_in.at[0], lists.at[0], meta_local.at[0])
    own_live = pltpu.make_async_copy(live_in, live.at[pl.ds(0, 1)], meta_local.at[1])
    own_lists.start()
    own_live.start()

    def first_tile(rel, o, s):
        return lax.rem(half_of(rel) + o, 2) * 4 + s * PIECE

    def tiles(rel, core, o, s):
        return pl.ds((rel + 2) * 16 + core * 8 + first_tile(rel, o, s), PIECE)

    def window_copy(kind, rel_src, rel_dst, o, s, target):
        src = tiles(rel_src, c, o, s)
        first = src.start - (rel_src + 2) * 16 + (rel_dst + 2) * 16
        return pltpu.make_async_remote_copy(
            src_ref=kv.at[src],
            dst_ref=kv.at[pl.ds(first, PIECE)],
            send_sem=win_send.at[kind, o, s],
            recv_sem=win_recv.at[kind, o, s],
            device_id=target,
            device_id_type=MESH,
        )

    def pass_on(kind, rel_src, rel_dst, o, s, target):
        copy = window_copy(kind, rel_src, rel_dst, o, s, target)
        copy.start()
        started.append(copy)

    def window_wait(kind, rel, core, o, s):
        dst = kv.at[tiles(rel, core, o, s)]
        pltpu.make_async_copy(dst, dst, win_recv.at[kind, o, s]).wait()

    def own(o, s):
        for p in range(PIECE):
            j = first_tile(0, o, s) + p
            arrived(0, j)
            arrived(1, j)
        pass_on(DN1, 0, -1, o, s, up)
        pass_on(UP1, 0, 1, o, s, down)
        pass_on(SB0, 0, 0, o, s, sibling)

    def then(o, s):
        window_wait(DN1, -1, c, o, s)
        pass_on(DN2, -1, -2, o, s, up)
        pass_on(SBD1, -1, -1, o, s, sibling)
        window_wait(UP1, 1, c, o, s)
        pass_on(UP2, 1, 2, o, s, down)
        pass_on(SBU1, 1, 1, o, s, sibling)

    def chain_tiles(rel, core, t, s, to):
        return kv.at[pl.ds((to + 2) * 16 + core * 8 + first_tile(rel, 1, s), PIECE), t]

    def chain(stage):
        for s in range(SUBS):
            for t, rel, step, target in ((0, 2 - stage, -1, up), (1, stage - 2, 1, down)):
                if stage == 0:
                    for e in range(PIECE):
                        dst = kv.at[(rel + 2) * 16 + c * 8 + first_tile(rel, 1, s) + e, t]
                        pltpu.make_async_copy(dst, dst, far_recv.at[s * PIECE + e, t]).wait()
                else:
                    dst = chain_tiles(rel, c, t, s, rel)
                    pltpu.make_async_copy(dst, dst, chain_recv.at[stage - 1, t, s]).wait()
                if stage < 4:
                    src, dst = chain_tiles(rel, c, t, s, rel), chain_tiles(rel, c, t, s, rel + step)
                    started.append(remote(src, dst, chain_send.at[stage, t, s], chain_recv.at[stage, t, s], target))
                if abs(rel) < 2:
                    share(stage, t, rel, s).start()
                else:
                    pl.when(c == (0 if rel == 2 else 1))(share(stage, t, rel, s).start)

    def share(stage, t, rel, s):
        src = chain_tiles(rel, c, t, s, rel)
        return pltpu.make_async_remote_copy(
            src_ref=src,
            dst_ref=src,
            send_sem=sib_send.at[stage, t, s],
            recv_sem=sib_recv.at[stage, t, s],
            device_id=sibling,
            device_id_type=MESH,
        )

    def shared(stage, t, rel, s):
        dst = chain_tiles(rel, 1 - c, t, s, rel)
        wait = pltpu.make_async_copy(dst, dst, sib_recv.at[stage, t, s]).wait
        if abs(rel) < 2:
            wait()
            share(stage, t, rel, s).wait_send()
        else:
            sender = c == (0 if rel == 2 else 1)
            pl.when(sender)(share(stage, t, rel, s).wait_send)
            pl.when(jnp.logical_not(sender))(wait)

    q_copies = [
        pltpu.make_async_remote_copy(
            src_ref=q_in.at[:, columns(h)],
            dst_ref=qs.at[g],
            send_sem=a2a_send.at[i, 2],
            recv_sem=a2a_recv.at[g, 2],
            device_id=(f, o),
            device_id_type=MESH,
        )
        for i, (o, h) in enumerate(others[:4])
    ]
    started.extend(q_copies)

    def q_far(*some):
        for i in some:
            q_copies[i].start()

    for s in range(SUBS):
        own(0, s)
    for i in range(4, 7):
        exchange(i, 2)
    chain(0)
    for s in range(SUBS):
        then(0, s)
    chain(1)
    q_far(0)
    chain(2)
    q_far(1)
    started.append(remote(lists_in, list_land, meta_send.at[0], meta_recv.at[0], across))
    started.append(remote(live_in, live_land, meta_send.at[1], meta_recv.at[1], across))
    chain(3)
    q_far(2, 3)
    chain(4)

    for o in (0,):
        for s in range(SUBS):
            window_wait(DN2, -2, c, o, s)

            @pl.when(c == 1)
            def _():
                window_copy(SBD2, -2, -2, o, s, sibling).start()

            window_wait(UP2, 2, c, o, s)

            @pl.when(c == 0)
            def _():
                window_copy(SBU2, 2, 2, o, s, sibling).start()

    for o in (0,):
        for s in range(SUBS):
            for kind, rel in ((SB0, 0), (SBD1, -1), (SBU1, 1)):
                window_wait(kind, rel, 1 - c, o, s)

            @pl.when(c == 0)
            def _():
                window_wait(SBD2, -2, 1, o, s)
                window_copy(SBU2, 2, 2, o, s, sibling).wait_send()

            @pl.when(c == 1)
            def _():
                window_wait(SBU2, 2, 0, o, s)
                window_copy(SBD2, -2, -2, o, s, sibling).wait_send()

    for stage in range(5):
        for s in range(SUBS):
            shared(stage, 0, 2 - stage, s)
            shared(stage, 1, stage - 2, s)

    pltpu.make_async_copy(list_land, list_land, meta_recv.at[0]).wait()
    pltpu.make_async_copy(live_land, live_land, meta_recv.at[1]).wait()
    own_lists.wait()
    own_live.wait()
    crossed_lists = pltpu.make_async_copy(list_land.at[0], lists.at[1], meta_local.at[2])
    crossed_live = pltpu.make_async_copy(live_land, live.at[pl.ds(1, 1)], meta_local.at[3])
    crossed_lists.start()
    crossed_live.start()
    crossed_lists.wait()
    crossed_live.wait()

    odd = lax.rem(x, 2)
    base = (m - 2) * 16
    factor = math.log2(math.e) / math.sqrt(DIM)

    def attend(i, carry):
        j, _ = owner(i)
        arrived(2, j)
        query = qs[j]
        ids = [jnp.clip(lists[odd, j, s] - base, 0, 79) for s in range(SLOTS)]
        count = live[odd, j]
        peak = jnp.full((TILE, 2 * TILE), -jnp.inf, jnp.float32)
        for s in range(0, SLOTS, 2):
            pair = jnp.concatenate([kv[ids[s], 0], kv[ids[s + 1], 0]], axis=0)
            raw = lax.dot_general(query, pair, (((1,), (1,)), ((), ())), preferred_element_type=jnp.float32)
            scores[s // 2] = raw
            peak = jnp.maximum(peak, raw)
        top = jnp.max(peak, axis=1, keepdims=True) * factor
        total = jnp.zeros((TILE, 2 * TILE), jnp.float32)
        acc = jnp.zeros((TILE, DIM), jnp.float32)
        lane = lax.broadcasted_iota(jnp.int32, (1, 2 * TILE), 1)
        for s in range(0, SLOTS, 2):
            dead = jnp.where(s + lax.div(lane, TILE) < count, 0.0, jnp.inf)
            weight = jnp.exp2(scores[s // 2] * factor - (top + dead))
            total = total + weight
            pair = jnp.concatenate([kv[ids[s], 1], kv[ids[s + 1], 1]], axis=0)
            acc = acc + jnp.dot(weight.astype(jnp.bfloat16), pair, preferred_element_type=jnp.float32)
        os[j] = (acc / jnp.sum(total, axis=1, keepdims=True)).astype(jnp.bfloat16)

        @pl.when(i < 7)
        def _():
            remote(os.at[j], out.at[:, columns(head)], out_send.at[j], out_recv.at[g], (f, j))

        @pl.when(i == 7)
        def _():
            pltpu.make_async_copy(os.at[j], out.at[:, columns(head)], out_recv.at[g]).start()

        return carry

    lax.fori_loop(0, 8, attend, 0)

    for copy in started:
        copy.wait_send()
    for o, _ in others:
        pltpu.make_async_copy(os.at[o], os.at[o], out_send.at[o]).wait()
    for o, h in others + [(g, head)]:
        dst = out.at[:, columns(h)]
        pltpu.make_async_copy(dst, dst, out_recv.at[o]).wait()


def body(queries, key_vectors, value_vectors, tile_lists, live_slots):
    dma = pltpu.SemaphoreType.DMA
    hbm = pl.BlockSpec(memory_space=pltpu.HBM)
    bf16, i32 = jnp.bfloat16, jnp.int32
    return pl.pallas_call(
        kernel,
        out_shape=jax.ShapeDtypeStruct(queries.shape, queries.dtype),
        in_specs=[hbm] * 5,
        out_specs=hbm,
        scratch_shapes=[
            pltpu.VMEM((80, 2, TILE, DIM), bf16),
            pltpu.VMEM((8, TILE, DIM), bf16),
            pltpu.VMEM((8, TILE, DIM), bf16),
            pltpu.VMEM((SLOTS // 2, TILE, 2 * TILE), jnp.float32),
            pltpu.VMEM(tile_lists.shape, i32),
            pltpu.VMEM(live_slots.shape, i32),
            pltpu.SMEM((2,) + tile_lists.shape[1:], i32),
            pltpu.SMEM((2, live_slots.shape[1]), i32),
            dma((7, 3)),
            dma((8, 3)),
            dma((9, 2, SUBS)),
            dma((9, 2, SUBS)),
            dma((8,)),
            dma((8,)),
            dma((2,)),
            dma((2,)),
            dma((4,)),
            dma((4, 2)),
            dma((4, 2)),
            dma((4, 2, SUBS)),
            dma((4, 2, SUBS)),
            dma((5, 2, SUBS)),
            dma((5, 2, SUBS)),
        ],
        compiler_params=pltpu.CompilerParams(
            collective_id=0, has_side_effects=True, vmem_limit_bytes=63 << 20
        ),
    )(queries, key_vectors, value_vectors, tile_lists, live_slots)


def solution(mesh):
    placed = (
        P(("frame", "head"), None),
        P(("frame", "head"), None),
        P(("frame", "head"), None),
        P("head", "frame", None),
        P("head", "frame"),
    )
    return jax.shard_map(
        body, mesh=mesh, in_specs=placed, out_specs=P(("frame", "head"), None), check_vma=False
    )
```
